32 devices in a mesh: seq: 8 (over z, y), fsdp: 4 (over x, core).
Axes of the slice: x: 2, y: 2, z: 4, core: 2. Of those that a mesh axis runs over, the one named last changes fastest.
Arguments:
- inputs: bfloat16 [4, 1024, 2048], P('fsdp', 'seq'), may hold values from -6 to 6
- qkv_weight: bfloat16 [2048, 4096], P(None, 'fsdp'), may hold values from -0.125 to 0.125
- gate_weight: bfloat16 [2048, 32], replicated, may hold values from -0.125 to 0.125
- conv_weight: bfloat16 [4, 4096], replicated, may hold values from -3 to 3
- head_rate: float32 [16], replicated, may hold values from 0 to 1, as said below
- dt_bias: float32 [16], replicated, may hold values from -2 to 1
- norm_gain: float32 [128], replicated, may hold values from 0.5 to 1.5
Outputs:
- output: bfloat16 [4, 1024, 2048], P('fsdp', 'seq')
The draws below stay inside these ranges and needn't reach their ends.
Inputs may be any that keep to these rules, and one draw needn't show every extreme that they name: `head_rate`: positive decay rates of the value heads.
All inputs are finite; a program needn't handle non-finite values.
Results may differ from the reference program's by a relative error of at most 0.0063.
Values may be sent and summed in bfloat16 or wider, within the bound.
No kernel may reach another device: no remote copies, remote signals or barrier semaphores. Data moves between devices by JAX's collectives and lax.ppermute only.
A program may use at most 192 MiB of HBM per device.

```python
import math
from functools import partial
import jax
import jax.numpy as jnp
from jax import lax

D = 2048
HEAD = 128
HK = 8
HV = 16
KERNEL = 4
GROUP = 64
SEQS = 4
LENGTH = 1024
CH = 4096


def draw_head_rate(key, part):
    first = jax.random.fold_in(key, 0)
    logs = jax.random.uniform(first, (HV,), jnp.float32, math.log(0.0001), math.log(0.1))
    return jnp.exp(logs).astype(jnp.float32)


def block_scale(own_key, dims, cuts, smallest, top_value):
    def one(position, shards_of):
        draws = jax.random.uniform(jax.random.fold_in(jax.random.fold_in(own_key, 6), position), (shards_of,), jnp.float32, smallest / len(cuts), top_value / len(cuts))
        return jnp.repeat(jnp.exp(draws), dims[position] // shards_of).reshape((-1,) + (1,) * (len(dims) - position - 1))

    loudness = one(*cuts[0])
    for cut in cuts[1:]:
        loudness = loudness * one(*cut)
    return loudness


def centred(rng, extent, scale, limit, pieces=(), held_as=jnp.bfloat16):
    values = scale * jax.random.normal(rng, extent, jnp.float32)
    if pieces:
        values = values * block_scale(rng, extent, pieces, -0.22, 0.18)
    return jnp.clip(values, -limit, limit).astype(held_as)


def setup_inputs(seed: int = 0) -> dict:
    key_list = jax.random.split(jax.random.key(seed), 8)
    inputs = centred(key_list[0], (SEQS, LENGTH, D), 1.0, 6.0, ((0, 4), (1, 8)))
    qkv_weight = centred(key_list[1], (D, CH), D ** -0.5, 0.125, ((1, 4),))
    gate_weight = centred(key_list[2], (D, 2 * HV), D ** -0.5, 0.125)
    conv_weight = centred(key_list[3], (KERNEL, CH), KERNEL ** -0.5, 3.0)
    head_rate = draw_head_rate(jax.random.fold_in(key_list[7], 71), 0)
    dt_bias = jnp.clip(jax.random.uniform(key_list[5], (HV,), jnp.float32, -2.0, 1.0), -2.0, 1.0)
    norm_gain = jnp.clip(1.0 + 0.1 * jax.random.normal(key_list[6], (HEAD,), jnp.float32), 0.5, 1.5)
    return {"inputs": inputs, "qkv_weight": qkv_weight, "gate_weight": gate_weight, "conv_weight": conv_weight, "head_rate": head_rate, "dt_bias": dt_bias, "norm_gain": norm_gain}


exact_products = lax.Precision.HIGHEST

def convolve(extended, conv_weight, length):
    running = jnp.zeros((length, extended.shape[1]), jnp.float32)
    for tap_index in range(conv_weight.shape[0]):
        running = running + conv_weight[tap_index].astype(jnp.float32) * extended[tap_index:tap_index + length].astype(jnp.float32)
    return jax.nn.silu(running)

def unit_rows(vectors):
    return vectors / jnp.sqrt(lax.optimization_barrier(jnp.sum(vectors * vectors, axis=-1, keepdims=True)) + 1e-06)

def head_inputs(activated, gates, head_rate, dt_bias):
    length = activated.shape[0]
    key_width = HK * HEAD
    blocks = length // GROUP
    query_heads = unit_rows(activated[:, :key_width].reshape(length, HK, HEAD)) * HEAD ** (-0.5)
    key_heads = unit_rows(activated[:, key_width:2 * key_width].reshape(length, HK, HEAD))
    value_heads = activated[:, 2 * key_width:].reshape(length, HV, HEAD)
    query_heads = jnp.repeat(query_heads, HV // HK, axis=1)
    key_heads = jnp.repeat(key_heads, HV // HK, axis=1)
    strength = jax.nn.sigmoid(gates[:, :HV])
    log_decay = -head_rate * jax.nn.softplus(gates[:, HV:] + dt_bias)

    def arrange(array):
        return jnp.transpose(array.reshape(blocks, GROUP, HV, HEAD), (2, 0, 1, 3))

    def arrange_flat(array):
        return jnp.transpose(array.reshape(blocks, GROUP, HV), (2, 0, 1))
    return (arrange(query_heads), arrange(key_heads), arrange(value_heads), arrange_flat(log_decay), arrange_flat(strength))

def group_parts(query_blocks, key_blocks, value_blocks, decay_blocks, strength_blocks):
    cumulative = jnp.cumsum(decay_blocks, axis=-1)
    spread = cumulative[..., :, None] - cumulative[..., None, :]
    row_index = jnp.arange(GROUP)[:, None]
    col_index = jnp.arange(GROUP)[None, :]
    strict = row_index > col_index
    within = row_index >= col_index
    key_key = jnp.einsum('hnid,hnjd->hnij', key_blocks, key_blocks, precision=exact_products)
    lower_part = jnp.where(strict, strength_blocks[..., :, None] * jnp.exp(jnp.where(strict, spread, 0.0)) * key_key, 0.0)
    system = lower_part + jnp.eye(GROUP, dtype=jnp.float32)
    scaled = jnp.concatenate([(strength_blocks * jnp.exp(cumulative))[..., None] * key_blocks, strength_blocks[..., None] * value_blocks], axis=-1)
    solved = lax.linalg.triangular_solve(system, scaled, left_side=True, lower=True, unit_diagonal=True)
    weighted_keys = solved[..., :HEAD]
    weighted_values = solved[..., HEAD:]
    query_key = jnp.einsum('hnid,hnjd->hnij', query_blocks, key_blocks, precision=exact_products)
    mixing = jnp.where(within, jnp.exp(jnp.where(within, spread, 0.0)) * query_key, 0.0)
    return (cumulative, weighted_keys, weighted_values, mixing)

def normalize(reads, norm_gain):
    square_mean = lax.optimization_barrier(jnp.mean(reads * reads, axis=-1, keepdims=True))
    scaled = reads / jnp.sqrt(square_mean + 1e-06) * norm_gain
    return jnp.transpose(scaled, (0, 2, 1, 3)).reshape(-1, HV * HEAD).astype(jnp.bfloat16)

def one_sequence(tokens, qkv_weight, gate_weight, conv_weight, head_rate, dt_bias, norm_gain):
    length = tokens.shape[0]
    mixed = jnp.dot(tokens.astype(jnp.float32), qkv_weight.astype(jnp.float32), preferred_element_type=jnp.float32).astype(jnp.bfloat16)
    gates = jnp.dot(tokens.astype(jnp.float32), gate_weight.astype(jnp.float32), preferred_element_type=jnp.float32)
    extended = jnp.concatenate([jnp.zeros((KERNEL - 1, mixed.shape[1]), jnp.bfloat16), mixed], axis=0)
    activated = convolve(extended, conv_weight, length)
    query_blocks, key_blocks, value_blocks, decay_blocks, strength_blocks = head_inputs(activated, gates, head_rate, dt_bias)
    cumulative, weighted_keys, weighted_values, mixing = group_parts(query_blocks, key_blocks, value_blocks, decay_blocks, strength_blocks)
    growth = jnp.exp(cumulative)
    trailing = jnp.exp(cumulative[..., -1:] - cumulative)

    def advance(state, items):
        query_c, key_c, wkey_c, wval_c, mix_c, grow_c, trail_c = items
        fresh = wval_c - jnp.einsum('hcd,hvd->hcv', wkey_c, state, precision=exact_products)
        reads = grow_c[..., None] * jnp.einsum('hcd,hvd->hcv', query_c, state, precision=exact_products)
        reads = reads + jnp.einsum('hij,hjv->hiv', mix_c, fresh, precision=exact_products)
        state = grow_c[:, -1, None, None] * state + jnp.einsum('hjv,hj,hjd->hvd', fresh, trail_c, key_c, precision=exact_products)
        return (state, reads)
    items = tuple((jnp.moveaxis(array, 1, 0) for array in (query_blocks, key_blocks, weighted_keys, weighted_values, mixing, growth, trailing)))
    start = jnp.zeros((HV, HEAD, HEAD), jnp.float32)
    reads = lax.scan(advance, start, items)[1]
    return normalize(reads, norm_gain)

def reference(inputs, qkv_weight, gate_weight, conv_weight, head_rate, dt_bias, norm_gain):
    single = partial(one_sequence, qkv_weight=qkv_weight, gate_weight=gate_weight, conv_weight=conv_weight, head_rate=head_rate, dt_bias=dt_bias, norm_gain=norm_gain)
    return lax.map(single, inputs)
```

```python
import jax
import jax.numpy as jnp
import numpy as np
from jax import lax
from jax.experimental import pallas as pl
from jax.experimental.pallas import tpu as pltpu
from jax.sharding import Mesh
from jax.sharding import PartitionSpec as P

HEAD = 128
HK = 8
HV = 16
KERNEL = 4
PAIR = 2
SPLIT = HK // PAIR
CHUNK = 128
BASE = 32
EXTRA = 16
RIM = 8
UNITS = HV // SPLIT
F32 = jnp.float32
BF16 = jnp.bfloat16
HIGHEST = lax.Precision.HIGHEST


def shifted(value, axes, pairs):
    return lax.ppermute(value, axes, pairs)


def swapped(value, axis, bit):
    count = lax.axis_size(axis)
    return lax.ppermute(value, axis, [(i, i ^ bit) for i in range(count)])


def dot(a, b):
    return jnp.dot(a, b, preferred_element_type=F32)


def halves(a):
    high = a.astype(BF16)
    return high, (a - high.astype(F32)).astype(BF16)


def dot3(a, b):
    return dot(a[0], b[0]) + (dot(a[0], b[1]) + dot(a[1], b[0]))


def split3(a):
    high = a.astype(BF16).astype(F32)
    rest = a - high
    middle = rest.astype(BF16).astype(F32)
    return high, middle, rest - middle


def iota(shape, dim):
    return lax.broadcasted_iota(jnp.int32, shape, dim)


def project_kernel(place, x0, x1, x2, x3, rims, gate_t, w_a, w_b, out, lhs, gates):
    step = pl.program_id(0)
    rows = x0.shape[0]
    me = place[0]

    @pl.when(step == 0)
    def _():
        for k, x in enumerate((x0, x1, x2, x3)):
            lhs[k * rows : (k + 1) * rows, :] = x[...]
        lhs[4 * rows :, :] = rims[...]
        raw = lax.dot_general(
            gate_t[...], lhs[: 4 * rows, :], (((1,), (1,)), ((), ())), preferred_element_type=F32
        )
        for part, value in enumerate(split3(raw)):
            for j in range(SPLIT):
                for k in range(4):
                    both = value[2 * j : 2 * j + 2, k * rows : (k + 1) * rows]
                    gates[j, k, part : part + 1, :] = jnp.concatenate([both[0:1], both[1:2]], axis=1)

    weights = jnp.concatenate([w_a[...], w_b[...]], axis=1)
    mixed = dot(lhs[...], weights)
    for k in range(4):
        target = jnp.bitwise_xor(me, k)
        out[0, target, :rows, :] = mixed[k * rows : (k + 1) * rows].astype(BF16)
        before = mixed[4 * rows + k * EXTRA : 4 * rows + (k + 1) * EXTRA]
        before = jnp.where(iota(before.shape, 0) < 3, gates[step, k], before)
        out[0, target, rows:, :] = before.astype(BF16)


def project(place, xs, rims, gate_t, weight):
    rows, depth = xs[0].shape
    width = 2 * HEAD
    whole = lambda shape: pl.BlockSpec(shape, lambda j, s: (0,) * len(shape))
    grid_spec = pltpu.PrefetchScalarGridSpec(
        num_scalar_prefetch=1,
        grid=(SPLIT,),
        in_specs=[whole((rows, depth))] * 4
        + [
            whole(rims.shape),
            whole(gate_t.shape),
            pl.BlockSpec((depth, HEAD), lambda j, s: (0, jnp.where(s[0] < 2, j, 2 * j))),
            pl.BlockSpec((depth, HEAD), lambda j, s: (0, jnp.where(s[0] < 2, SPLIT + j, 2 * j + 1))),
        ],
        out_specs=pl.BlockSpec((1, 4, rows + EXTRA, width), lambda j, s: (j, 0, 0, 0)),
        scratch_shapes=[
            pltpu.VMEM((4 * rows + 4 * EXTRA, depth), BF16),
            pltpu.VMEM((SPLIT, 4, EXTRA, width), F32),
        ],
    )
    return pl.pallas_call(
        project_kernel,
        grid_spec=grid_spec,
        out_shape=jax.ShapeDtypeStruct((SPLIT, 4, rows + EXTRA, width), BF16),
        name="project",
    )(place, *xs, rims, gate_t, weight, weight)


def base_inverse(lower):
    count = CHUNK // BASE
    tiles = BASE // 8
    lane_block = iota((8, CHUNK), 1) // BASE
    packed, result = [], []
    for t in range(tiles):
        tile = jnp.zeros((8, CHUNK), F32)
        for b in range(count):
            start = b * BASE + 8 * t
            tile = jnp.where(lane_block == b, lower[start : start + 8], tile)
        packed.append(tile)
        inside = iota((8, CHUNK), 1) % BASE
        result.append(jnp.where(inside == iota((8, CHUNK), 0) + 8 * t, 1.0, 0.0))
    for j in range(BASE - 1):
        row = jnp.broadcast_to(result[j // 8][j % 8 : j % 8 + 1], (8, CHUNK))
        source = lane_block * BASE + j
        for t in range((j + 1) // 8, tiles):
            column = jnp.take_along_axis(packed[t], source, axis=1)
            result[t] = result[t] - column * row
    side = jnp.concatenate(result, axis=0)
    block = iota((BASE, CHUNK), 1) // BASE
    return jnp.concatenate([jnp.where(block == b, side, 0.0) for b in range(count)], axis=0)


def inverse(lower):
    total = base_inverse(lower)
    row, column = iota((CHUNK, CHUNK), 0), iota((CHUNK, CHUNK), 1)
    size = BASE
    while size < CHUNK:
        inside = (row // (2 * size) == column // (2 * size)) & (row // size > column // size)
        corner = halves(jnp.where(inside, lower, 0.0))
        parts = halves(total)
        total = total - dot3(parts, halves(dot3(corner, parts)))
        size *= 2
    return total


def prepare_kernel(seg_product, place, rate, bias, message, taps, carry_out, add_out, final, *rest):
    if seg_product:
        product_out, tail, state, product = rest
    else:
        tail, state = rest
    step = pl.program_id(0)
    j = place[0]
    rows = CHUNK

    @pl.when(step == 0)
    def _():
        state[...] = jnp.zeros_like(state)
        for f in range(4):
            tail[f] = message[f, rows + EXTRA - RIM :, :].astype(F32)

    row, column = iota((rows, rows), 0), iota((rows, rows), 1)
    strict, within = row > column, row >= column
    eye = jnp.where(row == column, 1.0, 0.0)
    if seg_product:

        @pl.when(step == 0)
        def _():
            product[...] = jnp.broadcast_to(eye, product.shape)

    def activated(f, half, first):
        lanes = slice(half * HEAD, (half + 1) * HEAD)
        here = message[f, :rows, lanes].astype(F32)
        extended = jnp.concatenate([tail[f, :, lanes], here], axis=0)
        start = pl.multiple_of(first * HEAD, HEAD)
        weights = taps[:, pl.ds(start, HEAD)].astype(F32)
        total = jnp.zeros((rows, HEAD), F32)
        for tap in range(KERNEL):
            begin = RIM - (KERNEL - 1) + tap
            total = total + weights[tap : tap + 1] * extended[begin : begin + rows]
        tail[f, :, lanes] = here[rows - RIM :]
        return total / (1.0 + jnp.exp(-total))

    def unit(vectors):
        return vectors * lax.rsqrt(jnp.sum(vectors * vectors, axis=-1, keepdims=True) + 1e-06)

    decay_rows, strength_rows = [], []
    for u in range(UNITS):
        h, a = u // 2, u % 2
        head = 2 * (SPLIT * h + j) + a
        lanes = slice(a * HEAD, (a + 1) * HEAD)

        def gate(f):
            parts = message[f, rows : rows + EXTRA, lanes].astype(F32)
            return (parts[0:1] + parts[1:2]) + parts[2:3]

        strength_rows.append(1.0 / (1.0 + jnp.exp(-gate(h))))
        shift = gate(2 + h) + bias[head]
        soft = jnp.maximum(shift, 0.0) + jnp.log1p(jnp.exp(-jnp.abs(shift)))
        decay_rows.append(-rate[head] * soft)
    table = jnp.concatenate(decay_rows + strength_rows, axis=0)
    upper = jnp.where(row <= column, 1.0, 0.0)
    cum_rows = jnp.dot(table, upper, precision=HIGHEST, preferred_element_type=F32)
    lower_eye = jnp.concatenate([jnp.where(within, 1.0, 0.0), eye], axis=0)
    columns = lax.dot_general(
        lower_eye, table, (((1,), (1,)), ((), ())), precision=HIGHEST, preferred_element_type=F32
    )

    for h in range(PAIR):
        head = SPLIT * h + j
        query = unit(activated(0, h, head)) * HEAD ** (-0.5)
        key = unit(activated(1, h, HK + head))
        key_t = key.T
        key_t_parts = halves(key_t)
        both = halves(jnp.concatenate([key, query], axis=0))
        scores = dot3(both, key_t_parts)
        key_key, query_key = scores[:rows], scores[rows:]
        for a in range(2):
            u = 2 * h + a
            value = activated(2 + h, a, 2 * HK + 2 * head + a)
            cum_c = columns[:rows, u : u + 1]
            strength = columns[rows:, UNITS + u : UNITS + u + 1]
            cum_r = cum_rows[u : u + 1]
            last = cum_rows[u : u + 1, rows - 1 : rows]
            ratio = jnp.exp(jnp.minimum(cum_c - cum_r, 0.0))
            growth = jnp.exp(cum_c)
            trailing = jnp.exp(jnp.minimum(last - cum_r, 0.0))
            lower = jnp.where(strict, strength * ratio * key_key, 0.0)
            mixing = jnp.where(within, ratio * query_key, 0.0)
            solve = inverse(lower)
            scaled = jnp.concatenate([(strength * growth) * key, strength * value], axis=1)
            weighted = dot3(halves(solve), halves(scaled))
            left = jnp.concatenate([trailing * key_t, mixing], axis=0)
            mixed = dot3(halves(left), halves(weighted))
            carry = jnp.exp(last) * eye - mixed[:rows, :HEAD]
            read = growth * query - mixed[rows:, :HEAD]
            carry_out[0, u, :rows] = carry
            carry_out[0, u, rows:] = read
            add_out[0, u] = mixed[:, HEAD:]
            carry_parts = halves(carry)
            state[u] = dot3(carry_parts, halves(state[u])) + mixed[:rows, HEAD:]
            if seg_product:
                product[u] = dot3(carry_parts, halves(product[u]))

    @pl.when(step == pl.num_programs(0) - 1)
    def _():
        final[...] = state[...].astype(final.dtype)
        if seg_product:
            product_out[...] = product[...].astype(product_out.dtype)


def prepare(place, rate, bias, message, taps, seg_product):
    blocks = message.shape[0] // 4
    rows = message.shape[1] - EXTRA
    assert rows == CHUNK
    whole = lambda shape: pl.BlockSpec(shape, lambda b, *s: (0,) * len(shape))
    state_shape = (UNITS, HEAD, HEAD)
    out_shape = [
        jax.ShapeDtypeStruct((blocks, UNITS, 2 * rows, HEAD), F32),
        jax.ShapeDtypeStruct((blocks, UNITS, 2 * rows, HEAD), F32),
        jax.ShapeDtypeStruct(state_shape, BF16),
    ]
    stream = pl.BlockSpec((1, UNITS, 2 * rows, HEAD), lambda b, *s: (b, 0, 0, 0))
    out_specs = [stream, stream, whole(state_shape)]
    scratch = [pltpu.VMEM((4, RIM, 2 * HEAD), F32), pltpu.VMEM(state_shape, F32)]
    if seg_product:
        out_shape.append(jax.ShapeDtypeStruct(state_shape, F32))
        out_specs.append(whole(state_shape))
        scratch.append(pltpu.VMEM(state_shape, F32))
    grid_spec = pltpu.PrefetchScalarGridSpec(
        num_scalar_prefetch=3,
        grid=(blocks,),
        in_specs=[
            pl.BlockSpec((4, rows + EXTRA, 2 * HEAD), lambda b, *s: (b, 0, 0)),
            whole(taps.shape),
        ],
        out_specs=out_specs,
        scratch_shapes=scratch,
    )
    return pl.pallas_call(
        lambda *refs: prepare_kernel(seg_product, *refs),
        grid_spec=grid_spec,
        out_shape=out_shape,
        name="prepare",
    )(place, rate, bias, message, taps)


def read_kernel(place, carry, add, start, gain, out, state):
    @pl.when(pl.program_id(0) == 0)
    def _():
        state[...] = start[...].astype(F32)

    rows = CHUNK
    for u in range(UNITS):
        both = dot3(halves(carry[0, u]), halves(state[u])) + add[0, u]
        state[u] = both[:rows]
        reads = both[rows:]
        mean = jnp.mean(reads * reads, axis=-1, keepdims=True)
        out[0, :, u * HEAD : (u + 1) * HEAD] = (
            reads / jnp.sqrt(mean + 1e-06) * gain[...]
        ).astype(BF16)


def read(place, carry, add, start, gain):
    blocks, _, double, _ = carry.shape
    rows = double // 2
    whole = lambda shape: pl.BlockSpec(shape, lambda b, *s: (0,) * len(shape))
    stream = pl.BlockSpec((1, UNITS, double, HEAD), lambda b, *s: (b, 0, 0, 0))
    grid_spec = pltpu.PrefetchScalarGridSpec(
        num_scalar_prefetch=1,
        grid=(blocks,),
        in_specs=[stream, stream, whole(start.shape), whole(gain.shape)],
        out_specs=pl.BlockSpec(
            (1, rows, UNITS * HEAD), lambda b, s: (jnp.bitwise_xor(b, s[0]), 0, 0)
        ),
        scratch_shapes=[pltpu.VMEM(start.shape, F32)],
    )
    return pl.pallas_call(
        read_kernel,
        grid_spec=grid_spec,
        out_shape=jax.ShapeDtypeStruct((blocks, rows, UNITS * HEAD), BF16),
        name="read",
    )(place, carry, add, start, gain)


def assemble_kernel(place, *refs):
    out = refs[-1]
    width = 2 * HEAD
    for k, piece in enumerate(refs[:-1]):
        source = jnp.bitwise_xor(place[0], k)
        for h in range(PAIR):
            first = pl.multiple_of((h * SPLIT + source) * width, width)
            out[0, :, pl.ds(first, width)] = piece[:, h * width : (h + 1) * width]


def assemble(place, pieces):
    rows = pieces[0].shape[0]
    return pl.pallas_call(
        assemble_kernel,
        in_specs=[pl.BlockSpec(memory_space=pltpu.SMEM)]
        + [pl.BlockSpec(memory_space=pltpu.VMEM)] * len(pieces),
        out_specs=pl.BlockSpec(memory_space=pltpu.VMEM),
        out_shape=jax.ShapeDtypeStruct((1, rows, HV * HEAD), BF16),
        name="assemble",
    )(place, *pieces)


def messages_direct(tokens, qkv_weight, gate_weight, seq_count):
    me = lax.axis_index("fsdp")
    rim_rows = tokens[tokens.shape[0] - EXTRA :]
    far = swapped(tokens, "fsdp", 2)
    near = swapped(tokens, "fsdp", 1)
    rim_0 = shifted(rim_rows, ("seg", "sq"), [(i, i + 1) for i in range(seq_count - 1)])
    rim_2 = swapped(rim_0, "fsdp", 2)
    third = swapped(far, "fsdp", 1)
    rims_other = swapped(jnp.concatenate([rim_0, rim_2], axis=0), "fsdp", 1)
    rims = jnp.concatenate([rim_0, rims_other[:EXTRA], rim_2, rims_other[EXTRA:]], axis=0)
    share = 2 * HV // 4
    gate_t = lax.dynamic_slice_in_dim(gate_weight, me * share, share, 1).T
    place = me.astype(jnp.int32)[None]
    message = project(place, (tokens, near, far, third), rims, gate_t, qkv_weight)
    message = message.reshape((SPLIT * 4,) + message.shape[2:])
    return lax.all_to_all(message, ("sq", "fsdp"), 0, 0, tiled=True)


def messages_staged(tokens, qkv_weight, gate_weight, seq_count):
    length = tokens.shape[0]
    every = lax.all_gather(tokens, "fsdp", axis=0)
    mixed = jnp.einsum("ild,dc->ilc", every, qkv_weight, preferred_element_type=F32).astype(BF16)
    mixed = lax.all_to_all(mixed, "fsdp", 0, 2, tiled=True)[0]
    rim = shifted(
        mixed[length - RIM :], ("seg", "sq"), [(i, i + 1) for i in range(seq_count - 1)]
    )
    gates = jnp.dot(tokens, gate_weight, preferred_element_type=F32)
    high = lax.reduce_precision(gates, 8, 7)
    middle = lax.reduce_precision(gates - high, 8, 7)
    parts = jnp.stack([high, middle, (gates - high) - middle]).astype(BF16)
    parts = parts.reshape(3, length, 4, SPLIT, 2).transpose(3, 2, 0, 4, 1)
    parts = parts.reshape(SPLIT, 4, 3, 2 * length)

    def by_target(rows):
        count = rows.shape[0]
        query_key = rows[:, : 2 * HK * HEAD].reshape(count, 2, PAIR, SPLIT, HEAD)
        query_key = query_key.transpose(3, 1, 0, 2, 4).reshape(SPLIT, 2, count, 2 * HEAD)
        value = rows[:, 2 * HK * HEAD :].reshape(count, PAIR, SPLIT, 2 * HEAD)
        return jnp.concatenate([query_key, value.transpose(2, 1, 0, 3)], axis=1)

    blank = jnp.zeros((SPLIT, 4, EXTRA - RIM - 3, 2 * HEAD), BF16)
    message = jnp.concatenate([by_target(mixed), parts, blank, by_target(rim)], axis=2)
    message = lax.all_to_all(message, "sq", 0, 0, tiled=True)
    return message.reshape((SPLIT * 4,) + message.shape[2:])


def body(inputs, qkv_weight, gate_weight, conv_weight, head_rate, dt_bias, norm_gain):
    segments = lax.axis_size("seg")
    tokens = inputs[0]
    build = messages_direct if lax.axis_size("fsdp") == 4 else messages_staged
    message = build(tokens, qkv_weight, gate_weight, segments * SPLIT)
    place = lax.axis_index("sq").astype(jnp.int32)[None]
    outs = prepare(place, head_rate, dt_bias, message, conv_weight, segments > 2)
    carry, add, final = outs[:3]
    onward = [(i, i + 1) for i in range(segments - 1)]
    if segments == 1:
        start = jnp.zeros_like(final)
    elif segments == 2:
        start = shifted(final, "seg", onward)
    else:
        start = jnp.zeros_like(final)
        for _ in range(segments - 1):
            ahead = jnp.einsum("hij,hjk->hik", outs[3], start.astype(F32), precision=HIGHEST)
            start = shifted((ahead + final.astype(F32)).astype(BF16), "seg", onward)
    pieces = read(place, carry, add, start, norm_gain[None])
    received = [pieces[0]] + [swapped(pieces[k], "sq", k) for k in range(1, SPLIT)]
    return assemble(place, received)


def solution(mesh):
    seq, fsdp = mesh.shape["seq"], mesh.shape["fsdp"]
    parts = Mesh(mesh.devices.reshape(seq // SPLIT, SPLIT, fsdp), ("seg", "sq", "fsdp"))
    split = P("fsdp", ("seg", "sq"), None)
    in_specs = (split, P(None, "fsdp"), P(), P(), P(), P(), P())
    return jax.shard_map(body, mesh=parts, in_specs=in_specs, out_specs=split, check_vma=False)
```

```python
import jax
import jax.numpy as jnp
from jax import lax
from jax.experimental import pallas as pl
from jax.experimental.pallas import tpu as pltpu
from jax.sharding import Mesh
from jax.sharding import PartitionSpec as P


HEAD = 128
HK = 8
HV = 16
KERNEL = 4
PAIR = 2
SPLIT = HK // PAIR
CHUNK = 128
BASE = 16
PROJECT_VMEM = 24 << 20
VMEM_LIMIT = 67_043_328
EXTRA = 16
RIM = 8
UNITS = HV // SPLIT
F32 = jnp.float32
BF16 = jnp.bfloat16
HIGHEST = lax.Precision.HIGHEST


def shifted(value, axes, pairs):
    return lax.ppermute(value, axes, pairs)


def swapped(value, axis, bit):
    count = lax.axis_size(axis)
    return lax.ppermute(value, axis, [(i, i ^ bit) for i in range(count)])


def dot(a, b):
    return jnp.dot(a, b, preferred_element_type=F32)


def halves(a):
    high = a.astype(BF16)
    return high, (a - high.astype(F32)).astype(BF16)


def dot3(a, b):
    right = jnp.concatenate([jnp.concatenate(b, axis=1), jnp.concatenate([b[0], jnp.zeros_like(b[0])], axis=1)], axis=0)
    both = dot(jnp.concatenate(a, axis=1), right)
    width = b[0].shape[1]
    return both[:, :width] + both[:, width:]


def split3(a):
    high = a.astype(BF16).astype(F32)
    rest = a - high
    middle = rest.astype(BF16).astype(F32)
    return high, middle, rest - middle


def iota(shape, dim):
    return lax.broadcasted_iota(jnp.int32, shape, dim)


def project_kernel(other, place, x0, x1, rim_0, rim_1, gate_t, weight, *rest):
    out, lhs, stage, sems = rest[-4:]
    rows = x0.shape[0]
    me = place[0]
    pair = 1 - me // 2 if other else me // 2
    contiguous = me >= 2

    lhs[:rows, :] = x0[...]
    lhs[rows : 2 * rows, :] = x1[...]
    lhs[2 * rows :, :] = jnp.concatenate([rim_0[...], rim_1[...]], axis=0)
    raw = lax.dot_general(
        gate_t[...], lhs[: 2 * rows, :], (((1,), (1,)), ((), ())), preferred_element_type=F32
    )
    parts = split3(raw)
    blank = jnp.zeros((EXTRA - RIM - 3, 2 * HEAD), F32)
    copies = []
    for j in range(SPLIT):
        lanes = [
            pl.multiple_of(jnp.where(contiguous, 2 * j + a, SPLIT * a + j) * HEAD, HEAD)
            for a in range(2)
        ]
        columns = jnp.concatenate([weight[:, pl.ds(lane, HEAD)] for lane in lanes], axis=1)
        mixed = dot(lhs[...], columns)
        for k in range(2):
            target = jnp.bitwise_xor(me % 2, k)
            stage[j, target, :rows, :] = mixed[k * rows : (k + 1) * rows].astype(BF16)
            tokens = slice(k * rows, (k + 1) * rows)
            gate = [
                jnp.concatenate([p[2 * j : 2 * j + 1, tokens], p[2 * j + 1 : 2 * j + 2, tokens]], 1)
                for p in parts
            ]
            before = mixed[2 * rows + k * RIM : 2 * rows + (k + 1) * RIM]
            stage[j, target, rows:, :] = jnp.concatenate(gate + [blank, before], axis=0).astype(BF16)
        copy = pltpu.make_async_copy(stage.at[j], out.at[j, pl.ds(2 * pair, 2)], sems.at[j])
        copy.start()
        copies.append(copy)
    for copy in copies:
        copy.wait()


def project(place, xs, rims, gate_t, weight, other, message):
    rows, depth = xs[0].shape
    width = weight.shape[1]
    operands = [place, *xs, *rims, gate_t, weight]
    in_specs = [pl.BlockSpec(memory_space=pltpu.SMEM)]
    in_specs += [pl.BlockSpec(memory_space=pltpu.VMEM)] * (len(operands) - 1)
    aliases = {}
    if message is not None:
        aliases = {len(operands): 0}
        operands.append(message)
        in_specs.append(pl.BlockSpec(memory_space=pl.ANY))
    block = (SPLIT, 2, rows + EXTRA, 2 * HEAD)
    return pl.pallas_call(
        lambda *refs: project_kernel(other, *refs),
        in_specs=in_specs,
        out_specs=pl.BlockSpec(memory_space=pl.ANY),
        out_shape=jax.ShapeDtypeStruct((SPLIT, 4, rows + EXTRA, 2 * HEAD), BF16),
        scratch_shapes=[
            pltpu.VMEM((2 * rows + 2 * RIM, depth), BF16),
            pltpu.VMEM(block, BF16),
            pltpu.SemaphoreType.DMA((SPLIT,)),
        ],
        input_output_aliases=aliases,
        cost_estimate=pl.CostEstimate(
            flops=4 * rows * depth * width,
            bytes_accessed=2 * weight.size + 8 * xs[0].size,
            transcendentals=0,
        ),
        compiler_params=pltpu.CompilerParams(vmem_limit_bytes=PROJECT_VMEM),
        name="project_other" if other else "project_own",
    )(*operands)


def base_inverses(lowers):
    count = CHUNK // BASE
    tiles = BASE // 8
    lane_block = iota((8, CHUNK), 1) // BASE
    inside = iota((8, CHUNK), 1) % BASE
    packed, results = [], []
    for lower in lowers:
        pack, result = [], []
        for t in range(tiles):
            tile = jnp.zeros((8, CHUNK), F32)
            for b in range(count):
                start = b * BASE + 8 * t
                tile = jnp.where(lane_block == b, lower[start : start + 8], tile)
            pack.append(tile)
            result.append(jnp.where(inside == iota((8, CHUNK), 0) + 8 * t, 1.0, 0.0))
        packed.append(pack)
        results.append(result)
    for j in range(BASE - 1):
        source = lane_block * BASE + j
        for pack, result in zip(packed, results):
            row = jnp.broadcast_to(result[j // 8][j % 8 : j % 8 + 1], (8, CHUNK))
            for t in range((j + 1) // 8, tiles):
                column = jnp.take_along_axis(pack[t], source, axis=1)
                result[t] = result[t] - column * row
    block = iota((BASE, CHUNK), 1) // BASE
    totals = []
    for result in results:
        side = jnp.concatenate(result, axis=0)
        totals.append(
            jnp.concatenate([jnp.where(block == b, side, 0.0) for b in range(count)], axis=0)
        )
    return totals


def inverses(lowers):
    totals = base_inverses(lowers)
    row, column = iota((CHUNK, CHUNK), 0), iota((CHUNK, CHUNK), 1)
    size = BASE
    while size < CHUNK:
        inside = (row // (2 * size) == column // (2 * size)) & (row // size > column // size)
        parts = [halves(total) for total in totals]
        corners = [halves(jnp.where(inside, lower, 0.0)) for lower in lowers]
        inner = [halves(dot3(c, p)) for c, p in zip(corners, parts)]
        totals = [t - dot3(p, i) for t, p, i in zip(totals, parts, inner)]
        size *= 2
    return totals


def prepare_kernel(seg_product, place, rate, bias, message, taps, carry_out, add_out, final, *rest):
    if seg_product:
        product_out, tail, state, product = rest
    else:
        tail, state = rest
    step = pl.program_id(0)
    j = place[0]
    rows = CHUNK

    @pl.when(step == 0)
    def _():
        state[...] = jnp.zeros_like(state)
        for f in range(4):
            tail[f] = message[f, rows + EXTRA - RIM :, :].astype(F32)

    row, column = iota((rows, rows), 0), iota((rows, rows), 1)
    strict, within = row > column, row >= column
    eye = jnp.where(row == column, 1.0, 0.0)
    if seg_product:

        @pl.when(step == 0)
        def _():
            product[...] = jnp.broadcast_to(eye, product.shape)

    def activated(f, half, first):
        lanes = slice(half * HEAD, (half + 1) * HEAD)
        here = message[f, :rows, lanes].astype(F32)
        extended = jnp.concatenate([tail[f, :, lanes], here], axis=0)
        start = pl.multiple_of(first * HEAD, HEAD)
        weights = taps[:, pl.ds(start, HEAD)].astype(F32)
        total = jnp.zeros((rows, HEAD), F32)
        for tap in range(KERNEL):
            begin = RIM - (KERNEL - 1) + tap
            total = total + weights[tap : tap + 1] * extended[begin : begin + rows]
        tail[f, :, lanes] = here[rows - RIM :]
        return total / (1.0 + jnp.exp(-total))

    def unit(vectors):
        return vectors * lax.rsqrt(jnp.sum(vectors * vectors, axis=-1, keepdims=True) + 1e-06)

    decay_rows, strength_rows = [], []
    for u in range(UNITS):
        h, a = u // 2, u % 2
        head = 2 * (SPLIT * h + j) + a
        lanes = slice(a * HEAD, (a + 1) * HEAD)

        def gate(f):
            parts = message[f, rows : rows + EXTRA, lanes].astype(F32)
            return (parts[0:1] + parts[1:2]) + parts[2:3]

        strength_rows.append(1.0 / (1.0 + jnp.exp(-gate(h))))
        shift = gate(2 + h) + bias[head]
        soft = jnp.maximum(shift, 0.0) + jnp.log1p(jnp.exp(-jnp.abs(shift)))
        decay_rows.append(-rate[head] * soft)
    table = jnp.concatenate(decay_rows + strength_rows, axis=0)
    upper = jnp.where(row <= column, 1.0, 0.0)
    cum_rows = jnp.dot(table, upper, precision=HIGHEST, preferred_element_type=F32)
    lower_eye = jnp.concatenate([jnp.where(within, 1.0, 0.0), eye], axis=0)
    columns = lax.dot_general(
        lower_eye, table, (((1,), (1,)), ((), ())), precision=HIGHEST, preferred_element_type=F32
    )

    heads = [SPLIT * h + j for h in range(PAIR)]
    queries = [unit(activated(0, h, heads[h])) * HEAD ** (-0.5) for h in range(PAIR)]
    keys = [unit(activated(1, h, HK + heads[h])) for h in range(PAIR)]
    keys_t = [key.T for key in keys]
    scores = [
        dot3(halves(jnp.concatenate([keys[h], queries[h]], axis=0)), halves(keys_t[h]))
        for h in range(PAIR)
    ]
    growths, strengths, lasts, lowers, mixings = [], [], [], [], []
    for u in range(UNITS):
        cum_c = columns[:rows, u : u + 1]
        strength = columns[rows:, UNITS + u : UNITS + u + 1]
        cum_r = cum_rows[u : u + 1]
        ratio = jnp.exp(jnp.minimum(cum_c - cum_r, 0.0))
        growths.append(jnp.exp(cum_c))
        strengths.append(strength)
        lasts.append(cum_rows[u : u + 1, rows - 1 : rows])
        lowers.append(jnp.where(strict, strength * ratio * scores[u // 2][:rows], 0.0))
        mixings.append(jnp.where(within, ratio * scores[u // 2][rows:], 0.0))
    solves = inverses(lowers)
    weighted = []
    for u in range(UNITS):
        h, a = u // 2, u % 2
        value = activated(2 + h, a, 2 * HK + 2 * heads[h] + a)
        scaled = jnp.concatenate(
            [(strengths[u] * growths[u]) * keys[h], strengths[u] * value], axis=1
        )
        weighted.append(halves(dot3(halves(solves[u]), halves(scaled))))
    mixed = []
    for u in range(UNITS):
        trailing = jnp.exp(jnp.minimum(lasts[u] - cum_rows[u : u + 1], 0.0))
        left = jnp.concatenate([trailing * keys_t[u // 2], mixings[u]], axis=0)
        mixed.append(dot3(halves(left), weighted[u]))
    for u in range(UNITS):
        carry = jnp.exp(lasts[u]) * eye - mixed[u][:rows, :HEAD]
        carry_out[0, u, :rows] = carry
        carry_out[0, u, rows:] = growths[u] * queries[u // 2] - mixed[u][rows:, :HEAD]
        add_out[0, u] = mixed[u][:, HEAD:]
        carry_parts = halves(carry)
        state[u] = dot3(carry_parts, halves(state[u])) + mixed[u][:rows, HEAD:]
        if seg_product:
            product[u] = dot3(carry_parts, halves(product[u]))

    @pl.when(step == pl.num_programs(0) - 1)
    def _():
        final[...] = state[...].astype(final.dtype)
        if seg_product:
            product_out[...] = product[...].astype(product_out.dtype)


def prepare(place, rate, bias, message, taps, seg_product):
    blocks = message.shape[0] // 4
    rows = message.shape[1] - EXTRA
    assert rows == CHUNK
    whole = lambda shape: pl.BlockSpec(shape, lambda b, *s: (0,) * len(shape))
    state_shape = (UNITS, HEAD, HEAD)
    out_shape = [
        jax.ShapeDtypeStruct((blocks, UNITS, 2 * rows, HEAD), F32),
        jax.ShapeDtypeStruct((blocks, UNITS, 2 * rows, HEAD), F32),
        jax.ShapeDtypeStruct(state_shape, BF16),
    ]
    stream = pl.BlockSpec((1, UNITS, 2 * rows, HEAD), lambda b, *s: (b, 0, 0, 0))
    out_specs = [stream, stream, whole(state_shape)]
    scratch = [pltpu.VMEM((4, RIM, 2 * HEAD), F32), pltpu.VMEM(state_shape, F32)]
    if seg_product:
        out_shape.append(jax.ShapeDtypeStruct(state_shape, F32))
        out_specs.append(whole(state_shape))
        scratch.append(pltpu.VMEM(state_shape, F32))
    grid_spec = pltpu.PrefetchScalarGridSpec(
        num_scalar_prefetch=3,
        grid=(blocks,),
        in_specs=[
            pl.BlockSpec((4, rows + EXTRA, 2 * HEAD), lambda b, *s: (b, 0, 0)),
            whole(taps.shape),
        ],
        out_specs=out_specs,
        scratch_shapes=scratch,
    )
    return pl.pallas_call(
        lambda *refs: prepare_kernel(seg_product, *refs),
        grid_spec=grid_spec,
        out_shape=out_shape,
        compiler_params=pltpu.CompilerParams(vmem_limit_bytes=VMEM_LIMIT),
        name="prepare",
    )(place, rate, bias, message, taps)


def read_kernel(place, carry, add, start, gain, *rest):
    outs, result, state = rest[:-2], rest[-2], rest[-1]

    @pl.when(pl.program_id(0) == 0)
    def _():
        state[...] = start[...].astype(F32)

    rows = CHUNK
    for u in range(UNITS):
        both = dot3(halves(carry[0, u]), halves(state[u])) + add[0, u]
        state[u] = both[:rows]
        reads = both[rows:]
        mean = jnp.mean(reads * reads, axis=-1, keepdims=True)
        result[:, u * HEAD : (u + 1) * HEAD] = (
            reads / jnp.sqrt(mean + 1e-06) * gain[...]
        ).astype(BF16)
    slot = jnp.bitwise_xor(pl.program_id(0), place[0])
    for k, out in enumerate(outs):

        @pl.when(slot == k)
        def _(out=out):
            out[...] = result[...]


def read(place, carry, add, start, gain):
    blocks, _, double, _ = carry.shape
    rows = double // 2
    whole = lambda shape: pl.BlockSpec(shape, lambda b, *s: (0,) * len(shape))
    stream = pl.BlockSpec((1, UNITS, double, HEAD), lambda b, *s: (b, 0, 0, 0))
    grid_spec = pltpu.PrefetchScalarGridSpec(
        num_scalar_prefetch=1,
        grid=(blocks,),
        in_specs=[stream, stream, whole(start.shape), whole(gain.shape)],
        out_specs=[whole((rows, UNITS * HEAD))] * blocks,
        scratch_shapes=[pltpu.VMEM((rows, UNITS * HEAD), BF16), pltpu.VMEM(start.shape, F32)],
    )
    return pl.pallas_call(
        read_kernel,
        grid_spec=grid_spec,
        out_shape=[jax.ShapeDtypeStruct((rows, UNITS * HEAD), BF16)] * blocks,
        compiler_params=pltpu.CompilerParams(vmem_limit_bytes=VMEM_LIMIT),
        name="read",
    )(place, carry, add, start, gain)


def assemble_kernel(place, *refs):
    out = refs[-1]
    width = 2 * HEAD
    for k, piece in enumerate(refs[:-1]):
        source = jnp.bitwise_xor(place[0], k)
        for h in range(PAIR):
            first = pl.multiple_of((h * SPLIT + source) * width, width)
            out[0, :, pl.ds(first, width)] = piece[:, h * width : (h + 1) * width]


def assemble(place, pieces):
    rows = pieces[0].shape[0]
    return pl.pallas_call(
        assemble_kernel,
        in_specs=[pl.BlockSpec(memory_space=pltpu.SMEM)]
        + [pl.BlockSpec(memory_space=pltpu.VMEM)] * len(pieces),
        out_specs=pl.BlockSpec(memory_space=pltpu.VMEM),
        out_shape=jax.ShapeDtypeStruct((1, rows, HV * HEAD), BF16),
        compiler_params=pltpu.CompilerParams(vmem_limit_bytes=VMEM_LIMIT),
        name="assemble",
    )(place, *pieces)


def messages_direct(tokens, qkv_weight, gate_weight, seq_count):
    me = lax.axis_index("fsdp")
    rim_rows = tokens[tokens.shape[0] - RIM :]
    far = swapped(tokens, "fsdp", 2)
    near = swapped(tokens, "fsdp", 1)
    rim_0 = shifted(rim_rows, ("seg", "sq"), [(i, i + 1) for i in range(seq_count - 1)])
    rim_1 = swapped(rim_0, "fsdp", 1)
    rim_2 = swapped(rim_0, "fsdp", 2)
    share = 2 * HV // 4
    gate_t = lax.dynamic_slice_in_dim(gate_weight, me * share, share, 1).T
    place = me.astype(jnp.int32)[None]
    message = project(
        place, (tokens, near), (rim_0, rim_1), gate_t, qkv_weight, False, None
    )
    third = swapped(far, "fsdp", 1)
    rim_3 = swapped(rim_2, "fsdp", 1)
    message = project(
        place, (far, third), (rim_2, rim_3), gate_t, qkv_weight, True, message
    )
    message = message.reshape((SPLIT * 4,) + message.shape[2:])
    return lax.all_to_all(message, ("sq", "fsdp"), 0, 0, tiled=True)


def messages_staged(tokens, qkv_weight, gate_weight, seq_count):
    length = tokens.shape[0]
    every = lax.all_gather(tokens, "fsdp", axis=0)
    mixed = jnp.einsum("ild,dc->ilc", every, qkv_weight, preferred_element_type=F32).astype(BF16)
    mixed = lax.all_to_all(mixed, "fsdp", 0, 2, tiled=True)[0]
    rim = shifted(
        mixed[length - RIM :], ("seg", "sq"), [(i, i + 1) for i in range(seq_count - 1)]
    )
    gates = jnp.dot(tokens, gate_weight, preferred_element_type=F32)
    high = lax.reduce_precision(gates, 8, 7)
    middle = lax.reduce_precision(gates - high, 8, 7)
    parts = jnp.stack([high, middle, (gates - high) - middle]).astype(BF16)
    parts = parts.reshape(3, length, 4, SPLIT, 2).transpose(3, 2, 0, 4, 1)
    parts = parts.reshape(SPLIT, 4, 3, 2 * length)

    def by_target(rows):
        count = rows.shape[0]
        query_key = rows[:, : 2 * HK * HEAD].reshape(count, 2, PAIR, SPLIT, HEAD)
        query_key = query_key.transpose(3, 1, 0, 2, 4).reshape(SPLIT, 2, count, 2 * HEAD)
        value = rows[:, 2 * HK * HEAD :].reshape(count, PAIR, SPLIT, 2 * HEAD)
        return jnp.concatenate([query_key, value.transpose(2, 1, 0, 3)], axis=1)

    blank = jnp.zeros((SPLIT, 4, EXTRA - RIM - 3, 2 * HEAD), BF16)
    message = jnp.concatenate([by_target(mixed), parts, blank, by_target(rim)], axis=2)
    message = lax.all_to_all(message, "sq", 0, 0, tiled=True)
    return message.reshape((SPLIT * 4,) + message.shape[2:])


def layer(inputs, qkv_weight, gate_weight, conv_weight, head_rate, dt_bias, norm_gain):
    segments = lax.axis_size("seg")
    tokens = inputs[0]
    build = messages_direct if lax.axis_size("fsdp") == 4 else messages_staged
    message = build(tokens, qkv_weight, gate_weight, segments * SPLIT)
    place = lax.axis_index("sq").astype(jnp.int32)[None]
    outs = prepare(place, head_rate, dt_bias, message, conv_weight, segments > 2)
    carry, add, final = outs[:3]
    onward = [(i, i + 1) for i in range(segments - 1)]
    if segments == 1:
        start = jnp.zeros_like(final)
    elif segments == 2:
        start = shifted(final, "seg", onward)
    else:
        start = jnp.zeros_like(final)
        for _ in range(segments - 1):
            ahead = jnp.einsum("hij,hjk->hik", outs[3], start.astype(F32), precision=HIGHEST)
            start = shifted((ahead + final.astype(F32)).astype(BF16), "seg", onward)
    pieces = read(place, carry, add, start, norm_gain[None])
    received = [pieces[0]] + [swapped(pieces[k], "sq", k) for k in range(1, SPLIT)]
    return assemble(place, received)


def solution(mesh):
    seq, fsdp = mesh.shape["seq"], mesh.shape["fsdp"]
    parts = Mesh(mesh.devices.reshape(seq // SPLIT, SPLIT, fsdp), ("seg", "sq", "fsdp"))
    split = P("fsdp", ("seg", "sq"), None)
    in_specs = (split, P(None, "fsdp"), P(), P(), P(), P(), P())
    return jax.shard_map(layer, mesh=parts, in_specs=in_specs, out_specs=split, check_vma=False)
```

```python
import jax
import jax.numpy as jnp
from jax import lax
from jax.experimental import pallas as pl
from jax.experimental.pallas import tpu as pltpu
from jax.sharding import Mesh
from jax.sharding import PartitionSpec as P


HEAD = 128
HK = 8
HV = 16
KERNEL = 4
PAIR = 2
SPLIT = HK // PAIR
CHUNK = 128
BASE = 16
PROJECT_VMEM = 24 << 20
VMEM_LIMIT = 24 << 20
GROUPED = 4
EXTRA = 16
RIM = 8
UNITS = HV // SPLIT
F32 = jnp.float32
BF16 = jnp.bfloat16
HIGHEST = lax.Precision.HIGHEST


def shifted(value, axes, pairs):
    return lax.ppermute(value, axes, pairs)


def swapped(value, axis, bit):
    count = lax.axis_size(axis)
    return lax.ppermute(value, axis, [(i, i ^ bit) for i in range(count)])


def dot(a, b):
    return jnp.dot(a, b, preferred_element_type=F32)


def halves(a):
    high = a.astype(BF16)
    return high, (a - high.astype(F32)).astype(BF16)


def dot3(a, b):
    right = jnp.concatenate([jnp.concatenate(b, axis=1), jnp.concatenate([b[0], jnp.zeros_like(b[0])], axis=1)], axis=0)
    both = dot(jnp.concatenate(a, axis=1), right)
    width = b[0].shape[1]
    return both[:, :width] + both[:, width:]


def split3(a):
    high = a.astype(BF16).astype(F32)
    rest = a - high
    middle = rest.astype(BF16).astype(F32)
    return high, middle, rest - middle


def iota(shape, dim):
    return lax.broadcasted_iota(jnp.int32, shape, dim)


def project_kernel(other, place, x0, x1, rim_0, rim_1, gate_t, weight, *rest):
    out, lhs, stage, sems = rest[-4:]
    rows = x0.shape[0]
    me = place[0]
    pair = 1 - me // 2 if other else me // 2
    contiguous = me >= 2

    lhs[:rows, :] = x0[...]
    lhs[rows : 2 * rows, :] = x1[...]
    lhs[2 * rows :, :] = jnp.concatenate([rim_0[...], rim_1[...]], axis=0)
    raw = lax.dot_general(
        gate_t[...], lhs[: 2 * rows, :], (((1,), (1,)), ((), ())), preferred_element_type=F32
    )
    parts = split3(raw)
    blank = jnp.zeros((EXTRA - RIM - 3, 2 * HEAD), F32)
    copies = []
    for j in range(SPLIT):
        lanes = [
            pl.multiple_of(jnp.where(contiguous, 2 * j + a, SPLIT * a + j) * HEAD, HEAD)
            for a in range(2)
        ]
        columns = jnp.concatenate([weight[:, pl.ds(lane, HEAD)] for lane in lanes], axis=1)
        mixed = dot(lhs[...], columns)
        for k in range(2):
            target = jnp.bitwise_xor(me % 2, k)
            stage[j, target, :rows, :] = mixed[k * rows : (k + 1) * rows].astype(BF16)
            tokens = slice(k * rows, (k + 1) * rows)
            gate = [
                jnp.concatenate([p[2 * j : 2 * j + 1, tokens], p[2 * j + 1 : 2 * j + 2, tokens]], 1)
                for p in parts
            ]
            before = mixed[2 * rows + k * RIM : 2 * rows + (k + 1) * RIM]
            stage[j, target, rows:, :] = jnp.concatenate(gate + [blank, before], axis=0).astype(BF16)
        copy = pltpu.make_async_copy(stage.at[j], out.at[j, pl.ds(2 * pair, 2)], sems.at[j])
        copy.start()
        copies.append(copy)
    for copy in copies:
        copy.wait()


def project(place, xs, rims, gate_t, weight, other, message):
    rows, depth = xs[0].shape
    width = weight.shape[1]
    operands = [place, *xs, *rims, gate_t, weight]
    in_specs = [pl.BlockSpec(memory_space=pltpu.SMEM)]
    in_specs += [pl.BlockSpec(memory_space=pltpu.VMEM)] * (len(operands) - 1)
    aliases = {}
    if message is not None:
        aliases = {len(operands): 0}
        operands.append(message)
        in_specs.append(pl.BlockSpec(memory_space=pl.ANY))
    block = (SPLIT, 2, rows + EXTRA, 2 * HEAD)
    return pl.pallas_call(
        lambda *refs: project_kernel(other, *refs),
        in_specs=in_specs,
        out_specs=pl.BlockSpec(memory_space=pl.ANY),
        out_shape=jax.ShapeDtypeStruct((SPLIT, 4, rows + EXTRA, 2 * HEAD), BF16),
        scratch_shapes=[
            pltpu.VMEM((2 * rows + 2 * RIM, depth), BF16),
            pltpu.VMEM(block, BF16),
            pltpu.SemaphoreType.DMA((SPLIT,)),
        ],
        input_output_aliases=aliases,
        cost_estimate=pl.CostEstimate(
            flops=4 * rows * depth * width,
            bytes_accessed=2 * weight.size + 8 * xs[0].size,
            transcendentals=0,
        ),
        compiler_params=pltpu.CompilerParams(vmem_limit_bytes=PROJECT_VMEM),
        name="project_other" if other else "project_own",
    )(*operands)


def base_inverses(lowers):
    count = CHUNK // BASE
    tiles = BASE // 8
    lane_block = iota((8, CHUNK), 1) // BASE
    inside = iota((8, CHUNK), 1) % BASE
    packed, results = [], []
    for lower in lowers:
        pack, result = [], []
        for t in range(tiles):
            tile = jnp.zeros((8, CHUNK), F32)
            for b in range(count):
                start = b * BASE + 8 * t
                tile = jnp.where(lane_block == b, lower[start : start + 8], tile)
            pack.append(tile)
            result.append(jnp.where(inside == iota((8, CHUNK), 0) + 8 * t, 1.0, 0.0))
        packed.append(pack)
        results.append(result)
    for j in range(BASE - 1):
        source = lane_block * BASE + j
        for pack, result in zip(packed, results):
            row = jnp.broadcast_to(result[j // 8][j % 8 : j % 8 + 1], (8, CHUNK))
            for t in range((j + 1) // 8, tiles):
                column = jnp.take_along_axis(pack[t], source, axis=1)
                result[t] = result[t] - column * row
    block = iota((BASE, CHUNK), 1) // BASE
    totals = []
    for result in results:
        side = jnp.concatenate(result, axis=0)
        totals.append(
            jnp.concatenate([jnp.where(block == b, side, 0.0) for b in range(count)], axis=0)
        )
    return totals


def inverses(lowers):
    totals = base_inverses(lowers)
    row, column = iota((CHUNK, CHUNK), 0), iota((CHUNK, CHUNK), 1)
    size = BASE
    while size < CHUNK:
        inside = (row // (2 * size) == column // (2 * size)) & (row // size > column // size)
        parts = [halves(total) for total in totals]
        corners = [halves(jnp.where(inside, lower, 0.0)) for lower in lowers]
        inner = [halves(dot3(c, p)) for c, p in zip(corners, parts)]
        totals = [t - dot3(p, i) for t, p, i in zip(totals, parts, inner)]
        size *= 2
    return totals


def activated(extended, slot, message, block, f, half, taps, first):
    rows = CHUNK
    lanes = slice(half * HEAD, (half + 1) * HEAD)
    rim = message[4 * block + f, rows:, lanes].astype(F32)
    before = message[4 * jnp.maximum(block - 1, 0) + f, rows - EXTRA : rows, lanes].astype(F32)
    extended[slot, :RIM] = jnp.where(block == 0, rim, before)[EXTRA - RIM :]
    extended[slot, RIM:] = message[4 * block + f, :rows, lanes].astype(F32)
    weights = taps[:, pl.ds(pl.multiple_of(first * HEAD, HEAD), HEAD)].astype(F32)
    total = jnp.zeros((rows, HEAD), F32)
    for tap in range(KERNEL):
        begin = RIM - (KERNEL - 1) + tap
        total = total + weights[tap : tap + 1] * extended[slot, begin : begin + rows]
    middle = 0.5 * total
    return middle + middle * jnp.tanh(middle)


def unit(vectors):
    return vectors * lax.rsqrt(jnp.sum(vectors * vectors, axis=-1, keepdims=True) + 1e-06)


def prepare_kernel(seg_product, place, rate, bias, taps, message_hbm, *rest):
    carry_out, add_out, high_out, low_out, ratio_out, growth_out, key_high, key_low = rest[:8]
    final = rest[8]
    if seg_product:
        product_out, message, extended, state, sems, product = rest[9:]
    else:
        message, extended, state, sems = rest[9:]
    j = place[0]
    rows = CHUNK
    blocks = carry_out.shape[0]

    def fetch(block):
        part = pl.ds(4 * block, 4)
        return pltpu.make_async_copy(message_hbm.at[part], message.at[part], sems.at[block])

    for block in range(blocks):
        fetch(block).start()

    row, column = iota((rows, rows), 0), iota((rows, rows), 1)
    strict, within = row > column, row >= column
    eye = jnp.where(row == column, 1.0, 0.0)
    upper = jnp.where(row <= column, 1.0, 0.0)
    lower_eye = jnp.concatenate([jnp.where(within, 1.0, 0.0), eye], axis=0)
    heads = [SPLIT * h + j for h in range(PAIR)]
    state[...] = jnp.zeros_like(state)
    if seg_product:
        product[...] = jnp.broadcast_to(eye, product.shape)

    def gate_tables(block):
        decay_rows, strength_rows = [], []
        for u in range(UNITS):
            h, a = u // 2, u % 2
            head = 2 * heads[h] + a
            lanes = slice(a * HEAD, (a + 1) * HEAD)

            def gate(f):
                parts = message[4 * block + f, rows : rows + EXTRA, lanes].astype(F32)
                return (parts[0:1] + parts[1:2]) + parts[2:3]

            strength_rows.append(1.0 / (1.0 + jnp.exp(-gate(h))))
            shift = gate(2 + h) + bias[head]
            soft = jnp.maximum(shift, 0.0) + jnp.log1p(jnp.exp(-jnp.abs(shift)))
            decay_rows.append(-rate[head] * soft)
        return jnp.concatenate(decay_rows + strength_rows, axis=0)

    def several(index, _):
        group = [GROUPED * index + i for i in range(GROUPED)]
        for block in group:
            fetch(block).wait()
        tables = jnp.concatenate([gate_tables(block) for block in group], axis=0)
        sums = jnp.dot(tables, upper, precision=HIGHEST, preferred_element_type=F32)
        turned = lax.dot_general(
            lower_eye, tables, (((1,), (1,)), ((), ())), precision=HIGHEST, preferred_element_type=F32
        )
        keys, keys_t, scores = [], [], []
        for i, block in enumerate(group):
            for h in range(PAIR):
                slot = (PAIR + UNITS) * i + h
                key = unit(activated(extended, slot, message, block, 1, h, taps, HK + heads[h]))
                keys.append(key)
                keys_t.append(key.T)
                parts = halves(keys_t[-1])
                key_high[block, h], key_low[block, h] = parts
                scores.append(dot3(halves(key), parts))
        growths, strengths, lasts, trailings, lowers = [], [], [], [], []
        for i, block in enumerate(group):
            growth_all = jnp.exp(turned[:rows, 2 * UNITS * i : 2 * UNITS * (i + 1)])
            growth_out[block] = growth_all
            for u in range(UNITS):
                at = 2 * UNITS * i + u
                cum_c = turned[:rows, at : at + 1]
                strength = turned[rows:, at + UNITS : at + UNITS + 1]
                cum_r = sums[at : at + 1]
                last = sums[at : at + 1, rows - 1 : rows]
                ratio = jnp.where(within, jnp.exp(jnp.minimum(cum_c - cum_r, 0.0)), 0.0)
                ratio_out[block, u] = ratio
                growths.append(growth_all[:, u : u + 1])
                strengths.append(strength)
                lasts.append(last)
                trailings.append(jnp.exp(jnp.minimum(last - cum_r, 0.0)))
                score = scores[PAIR * i + u // 2]
                lowers.append(jnp.where(strict, strength * ratio * score, 0.0))
        solves = inverses(lowers)
        weighted = []
        for i, block in enumerate(group):
            for u in range(UNITS):
                h, a, at = u // 2, u % 2, UNITS * i + u
                slot = (PAIR + UNITS) * i + PAIR + u
                first = 2 * HK + 2 * heads[h] + a
                value = activated(extended, slot, message, block, 2 + h, a, taps, first)
                scaled = jnp.concatenate(
                    [(strengths[at] * growths[at]) * keys[PAIR * i + h], strengths[at] * value],
                    axis=1,
                )
                weighted.append(halves(dot3(halves(solves[at]), halves(scaled))))
                high_out[block, u], low_out[block, u] = weighted[at]
        carries, adds = [], []
        for i, block in enumerate(group):
            for u in range(UNITS):
                at = UNITS * i + u
                left = trailings[at] * keys_t[PAIR * i + u // 2]
                mixed = dot3(halves(left), weighted[at])
                carry = jnp.exp(lasts[at]) * eye - mixed[:, :HEAD]
                carry_out[block, u] = carry
                add_out[block, u] = mixed[:, HEAD:]
                carries.append(halves(carry))
                adds.append(mixed[:, HEAD:])
        for i in range(GROUPED):
            for u in range(UNITS):
                at = UNITS * i + u
                state[u] = dot3(carries[at], halves(state[u])) + adds[at]
                if seg_product:
                    product[u] = dot3(carries[at], halves(product[u]))
        return 0

    lax.fori_loop(0, blocks // GROUPED, several, 0)
    final[...] = state[...].astype(final.dtype)
    if seg_product:
        product_out[...] = product[...].astype(product_out.dtype)


def prepare(place, rate, bias, message, taps, seg_product):
    blocks = message.shape[0] // 4
    rows = message.shape[1] - EXTRA
    assert rows == CHUNK
    state_shape = (UNITS, HEAD, HEAD)
    streams = [
        (state_shape, F32),
        (state_shape, F32),
        ((UNITS, rows, 2 * HEAD), BF16),
        ((UNITS, rows, 2 * HEAD), BF16),
        ((UNITS, rows, rows), F32),
        ((rows, 2 * UNITS), F32),
        ((PAIR, HEAD, rows), BF16),
        ((PAIR, HEAD, rows), BF16),
    ]
    out_shape = [jax.ShapeDtypeStruct((blocks,) + shape, dtype) for shape, dtype in streams]
    out_shape.append(jax.ShapeDtypeStruct(state_shape, BF16))
    scratch = [
        pltpu.VMEM(message.shape, BF16),
        pltpu.VMEM(((PAIR + UNITS) * GROUPED, RIM + rows, HEAD), F32),
        pltpu.VMEM(state_shape, F32),
        pltpu.SemaphoreType.DMA((blocks,)),
    ]
    if seg_product:
        out_shape.append(jax.ShapeDtypeStruct(state_shape, F32))
        scratch.append(pltpu.VMEM(state_shape, F32))
    scalars = pl.BlockSpec(memory_space=pltpu.SMEM)
    vectors = pl.BlockSpec(memory_space=pltpu.VMEM)
    return pl.pallas_call(
        lambda *refs: prepare_kernel(seg_product, *refs),
        in_specs=[scalars] * 3 + [vectors, pl.BlockSpec(memory_space=pl.ANY)],
        out_specs=[vectors] * len(out_shape),
        out_shape=out_shape,
        scratch_shapes=scratch,
        compiler_params=pltpu.CompilerParams(vmem_limit_bytes=VMEM_LIMIT),
        name="prepare",
    )(place, rate, bias, taps, message)


def local_kernel(place, message, taps, high, low, ratio, growth, key_high, key_low, *rest):
    query_out, base_out, extended = rest
    heads = [SPLIT * h + place[0] for h in range(PAIR)]

    def one(block, _):
        queries, scores = [], []
        for h in range(PAIR):
            vectors = unit(activated(extended, h, message, block, 0, h, taps, heads[h]))
            queries.append(vectors * HEAD ** (-0.5))
            scores.append(dot3(halves(queries[h]), (key_high[block, h], key_low[block, h])))
        mixed = []
        for u in range(UNITS):
            mixing = ratio[block, u] * scores[u // 2]
            mixed.append(dot3(halves(mixing), (high[block, u], low[block, u])))
        for u in range(UNITS):
            query_out[block, u] = (
                growth[block, :, u : u + 1] * queries[u // 2] - mixed[u][:, :HEAD]
            )
            base_out[block, u] = mixed[u][:, HEAD:]
        return 0

    lax.fori_loop(0, query_out.shape[0], one, 0)


def local(place, message, taps, parts):
    blocks = message.shape[0] // 4
    rows = message.shape[1] - EXTRA
    shape = (blocks, UNITS, rows, HEAD)
    vectors = pl.BlockSpec(memory_space=pltpu.VMEM)
    flops = blocks * UNITS * 2 * 3 * rows * rows * 3 * HEAD
    return pl.pallas_call(
        local_kernel,
        in_specs=[pl.BlockSpec(memory_space=pltpu.SMEM)] + [vectors] * (2 + len(parts)),
        out_specs=[vectors, vectors],
        out_shape=[jax.ShapeDtypeStruct(shape, F32)] * 2,
        scratch_shapes=[pltpu.VMEM((PAIR, RIM + rows, HEAD), F32)],
        cost_estimate=pl.CostEstimate(
            flops=flops, bytes_accessed=12 << 20, transcendentals=message.size
        ),
        compiler_params=pltpu.CompilerParams(vmem_limit_bytes=VMEM_LIMIT),
        name="local",
    )(place, message, taps, *parts)


def read_kernel(place, carry, add, query, base, start, gain, *rest):
    outs, state = rest[:-1], rest[-1]
    state[...] = start[...].astype(F32)

    def one(block, _):
        results = []
        for u in range(UNITS):
            left = jnp.concatenate([carry[block, u], query[block, u]], axis=0)
            both = dot3(halves(left), halves(state[u]))
            state[u] = both[:HEAD] + add[block, u]
            reads = both[HEAD:] + base[block, u]
            mean = jnp.mean(reads * reads, axis=-1, keepdims=True)
            results.append((reads / jnp.sqrt(mean + 1e-06) * gain[...]).astype(BF16))
        slot = jnp.bitwise_xor(block, place[0])
        for k, out in enumerate(outs):

            @pl.when(slot == k)
            def _(out=out):
                for u in range(UNITS):
                    out[:, u * HEAD : (u + 1) * HEAD] = results[u]

        return 0

    lax.fori_loop(0, carry.shape[0], one, 0)


def read(place, carry, add, query, base, start, gain):
    blocks, _, rows, _ = query.shape
    vectors = pl.BlockSpec(memory_space=pltpu.VMEM)
    return pl.pallas_call(
        read_kernel,
        in_specs=[pl.BlockSpec(memory_space=pltpu.SMEM)] + [vectors] * 6,
        out_specs=[vectors] * blocks,
        out_shape=[jax.ShapeDtypeStruct((rows, UNITS * HEAD), BF16)] * blocks,
        scratch_shapes=[pltpu.VMEM(start.shape, F32)],
        compiler_params=pltpu.CompilerParams(vmem_limit_bytes=VMEM_LIMIT),
        name="read",
    )(place, carry, add, query, base, start, gain)


def assemble_kernel(place, *refs):
    out = refs[-1]
    width = 2 * HEAD
    for k, piece in enumerate(refs[:-1]):
        source = jnp.bitwise_xor(place[0], k)
        for h in range(PAIR):
            first = pl.multiple_of((h * SPLIT + source) * width, width)
            out[0, :, pl.ds(first, width)] = piece[:, h * width : (h + 1) * width]


def assemble(place, pieces):
    rows = pieces[0].shape[0]
    return pl.pallas_call(
        assemble_kernel,
        in_specs=[pl.BlockSpec(memory_space=pltpu.SMEM)]
        + [pl.BlockSpec(memory_space=pltpu.VMEM)] * len(pieces),
        out_specs=pl.BlockSpec(memory_space=pltpu.VMEM),
        out_shape=jax.ShapeDtypeStruct((1, rows, HV * HEAD), BF16),
        compiler_params=pltpu.CompilerParams(vmem_limit_bytes=VMEM_LIMIT),
        name="assemble",
    )(place, *pieces)


def messages_direct(tokens, qkv_weight, gate_weight, seq_count):
    me = lax.axis_index("fsdp")
    rim_rows = tokens[tokens.shape[0] - RIM :]
    far = swapped(tokens, "fsdp", 2)
    near = swapped(tokens, "fsdp", 1)
    rim_0 = shifted(rim_rows, ("seg", "sq"), [(i, i + 1) for i in range(seq_count - 1)])
    rim_1 = swapped(rim_0, "fsdp", 1)
    rim_2 = swapped(rim_0, "fsdp", 2)
    share = 2 * HV // 4
    gate_t = lax.dynamic_slice_in_dim(gate_weight, me * share, share, 1).T
    place = me.astype(jnp.int32)[None]
    message = project(
        place, (tokens, near), (rim_0, rim_1), gate_t, qkv_weight, False, None
    )
    third = swapped(far, "fsdp", 1)
    rim_3 = swapped(rim_2, "fsdp", 1)
    message = project(
        place, (far, third), (rim_2, rim_3), gate_t, qkv_weight, True, message
    )
    message = message.reshape((SPLIT * 4,) + message.shape[2:])
    return lax.all_to_all(message, ("sq", "fsdp"), 0, 0, tiled=True)


def messages_staged(tokens, qkv_weight, gate_weight, seq_count):
    length = tokens.shape[0]
    every = lax.all_gather(tokens, "fsdp", axis=0)
    mixed = jnp.einsum("ild,dc->ilc", every, qkv_weight, preferred_element_type=F32).astype(BF16)
    mixed = lax.all_to_all(mixed, "fsdp", 0, 2, tiled=True)[0]
    rim = shifted(
        mixed[length - RIM :], ("seg", "sq"), [(i, i + 1) for i in range(seq_count - 1)]
    )
    gates = jnp.dot(tokens, gate_weight, preferred_element_type=F32)
    high = lax.reduce_precision(gates, 8, 7)
    middle = lax.reduce_precision(gates - high, 8, 7)
    parts = jnp.stack([high, middle, (gates - high) - middle]).astype(BF16)
    parts = parts.reshape(3, length, 4, SPLIT, 2).transpose(3, 2, 0, 4, 1)
    parts = parts.reshape(SPLIT, 4, 3, 2 * length)

    def by_target(rows):
        count = rows.shape[0]
        query_key = rows[:, : 2 * HK * HEAD].reshape(count, 2, PAIR, SPLIT, HEAD)
        query_key = query_key.transpose(3, 1, 0, 2, 4).reshape(SPLIT, 2, count, 2 * HEAD)
        value = rows[:, 2 * HK * HEAD :].reshape(count, PAIR, SPLIT, 2 * HEAD)
        return jnp.concatenate([query_key, value.transpose(2, 1, 0, 3)], axis=1)

    blank = jnp.zeros((SPLIT, 4, EXTRA - RIM - 3, 2 * HEAD), BF16)
    message = jnp.concatenate([by_target(mixed), parts, blank, by_target(rim)], axis=2)
    message = lax.all_to_all(message, "sq", 0, 0, tiled=True)
    return message.reshape((SPLIT * 4,) + message.shape[2:])


def layer(inputs, qkv_weight, gate_weight, conv_weight, head_rate, dt_bias, norm_gain):
    segments = lax.axis_size("seg")
    tokens = inputs[0]
    build = messages_direct if lax.axis_size("fsdp") == 4 else messages_staged
    message = build(tokens, qkv_weight, gate_weight, segments * SPLIT)
    place = lax.axis_index("sq").astype(jnp.int32)[None]
    outs = prepare(place, head_rate, dt_bias, message, conv_weight, segments > 2)
    carry, add, parts, final = outs[0], outs[1], outs[2:8], outs[8]
    onward = [(i, i + 1) for i in range(segments - 1)]
    start = jnp.zeros_like(final)
    if segments == 2:
        start = shifted(final, "seg", onward)
    elif segments > 2:
        for _ in range(segments - 1):
            ahead = jnp.einsum("hij,hjk->hik", outs[9], start.astype(F32), precision=HIGHEST)
            start = shifted((ahead + final.astype(F32)).astype(BF16), "seg", onward)
    query, base = local(place, message, conv_weight, parts)
    pieces = read(place, carry, add, query, base, start, norm_gain[None])
    received = [pieces[0]] + [swapped(pieces[k], "sq", k) for k in range(1, SPLIT)]
    return assemble(place, received)


def solution(mesh):
    seq, fsdp = mesh.shape["seq"], mesh.shape["fsdp"]
    parts = Mesh(mesh.devices.reshape(seq // SPLIT, SPLIT, fsdp), ("seg", "sq", "fsdp"))
    split = P("fsdp", ("seg", "sq"), None)
    in_specs = (split, P(None, "fsdp"), P(), P(), P(), P(), P())
    return jax.shard_map(layer, mesh=parts, in_specs=in_specs, out_specs=split, check_vma=False)
```

```python
import jax
import jax.numpy as jnp
from jax import lax
from jax.experimental import pallas as pl
from jax.experimental.pallas import tpu as pltpu
from jax.sharding import Mesh
from jax.sharding import PartitionSpec as P


HEAD = 128
HK = 8
HV = 16
KERNEL = 4
PAIR = 2
SPLIT = HK // PAIR
CHUNK = 128
BASE = 16
PROJECT_VMEM = 24 << 20
VMEM_LIMIT = 24 << 20
GROUPED = 4
EXTRA = 8
RIM = 8
UNITS = HV // SPLIT
F32 = jnp.float32
BF16 = jnp.bfloat16
HIGHEST = lax.Precision.HIGHEST


def shifted(value, axes, pairs):
    return lax.ppermute(value, axes, pairs)


def swapped(value, axis, bit):
    count = lax.axis_size(axis)
    return lax.ppermute(value, axis, [(i, i ^ bit) for i in range(count)])


def in_hbm(value):
    return pltpu.with_memory_space_constraint(value, pltpu.HBM)


def dot(a, b):
    return jnp.dot(a, b, preferred_element_type=F32)


def halves(a):
    high = a.astype(BF16)
    return high, (a - high.astype(F32)).astype(BF16)


def dot3(a, b):
    right = jnp.concatenate([jnp.concatenate(b, axis=1), jnp.concatenate([b[0], jnp.zeros_like(b[0])], axis=1)], axis=0)
    both = dot(jnp.concatenate(a, axis=1), right)
    width = b[0].shape[1]
    return both[:, :width] + both[:, width:]


def split3(a):
    high = a.astype(BF16).astype(F32)
    rest = a - high
    middle = rest.astype(BF16).astype(F32)
    return high, middle, rest - middle


def iota(shape, dim):
    return lax.broadcasted_iota(jnp.int32, shape, dim)


def project_kernel(other, place, x0, x1, rim_0, rim_1, gate_hbm, weight_hbm, *rest):
    rows = x0.shape[0]
    me = place[0]
    pair = 1 - me // 2 if other else me // 2
    contiguous = me >= 2
    loads = []

    def lane(j, a):
        return pl.multiple_of(jnp.where(contiguous, 2 * j + a, SPLIT * a + j) * HEAD, HEAD)

    def load(source, target, sem):
        copy = pltpu.make_async_copy(source, target, sem)
        copy.start()
        loads.append(copy)

    if other:
        out, lhs, stage, gates, sems = rest[-5:]
        weight, gate_t = weight_hbm, gate_hbm
        lhs[:rows, :] = x0[...]
    else:
        out, weight, gate_t, lhs, stage, gates, sems, load_sems = rest
        load(x0, lhs.at[pl.ds(0, rows)], load_sems.at[0])
        load(gate_hbm, gate_t, load_sems.at[1])
        for j in range(SPLIT):
            for a in range(2):
                part = pl.ds(lane(j, a), HEAD)
                load(weight_hbm.at[:, part], weight.at[:, part], load_sems.at[2 + 2 * j + a])
    lhs[rows : 2 * rows, :] = x1[...]
    lhs[2 * rows :, :] = jnp.concatenate([rim_0[...], rim_1[...]], axis=0)
    for copy in loads[:2]:
        copy.wait()
    gates[...] = lax.dot_general(
        gate_t[...], lhs[: 2 * rows, :], (((1,), (1,)), ((), ())), preferred_element_type=F32
    )
    share = gate_t.shape[0] // 4
    parts = split3(gates[pl.ds(pl.multiple_of(me * share, share), share), :])
    index = iota((RIM, 2 * HEAD), 0)
    copies = []
    for j in range(SPLIT):
        for copy in loads[2 + 2 * j : 4 + 2 * j]:
            copy.wait()
        columns = jnp.concatenate([weight[:, pl.ds(lane(j, a), HEAD)] for a in range(2)], axis=1)
        mixed = dot(lhs[...], columns)
        for k in range(2):
            target = jnp.bitwise_xor(me % 2, k)
            stage[j, target, :rows, :] = mixed[k * rows : (k + 1) * rows].astype(BF16)
            tokens = slice(k * rows, (k + 1) * rows)
            tail = mixed[2 * rows + k * RIM : 2 * rows + (k + 1) * RIM]
            for part in range(3):
                gate = [parts[part][2 * j + a : 2 * j + a + 1, tokens] for a in range(2)]
                tail = jnp.where(index == part, jnp.concatenate(gate, axis=1), tail)
            stage[j, target, rows:, :] = tail.astype(BF16)
        copy = pltpu.make_async_copy(stage.at[j], out.at[j, pl.ds(2 * pair, 2)], sems.at[j])
        copy.start()
        copies.append(copy)
    for copy in copies:
        copy.wait()


def project(place, xs, rims, gate_t, weight, message):
    other = message is not None
    rows, depth = xs[0].shape
    width = weight.shape[1]
    vectors, anywhere = pl.BlockSpec(memory_space=pltpu.VMEM), pl.BlockSpec(memory_space=pl.ANY)
    operands = [place, *xs, *rims, gate_t, weight]
    first = vectors if other else pl.BlockSpec(memory_space=pltpu.HBM)
    in_specs = [pl.BlockSpec(memory_space=pltpu.SMEM), first] + [vectors] * 3 + [first] * 2
    message_shape = (SPLIT, 4, rows + EXTRA, 2 * HEAD)
    out_shape = [jax.ShapeDtypeStruct(message_shape, BF16)]
    out_specs = [anywhere]
    scratch = [
        pltpu.VMEM((2 * rows + 2 * RIM, depth), BF16),
        pltpu.VMEM((SPLIT, 2, rows + EXTRA, 2 * HEAD), BF16),
        pltpu.VMEM((gate_t.shape[0], 2 * rows), F32),
        pltpu.SemaphoreType.DMA((SPLIT,)),
    ]
    aliases = {}
    if other:
        aliases = {len(operands): 0}
        operands.append(message)
        in_specs.append(anywhere)
    else:
        out_shape += [jax.ShapeDtypeStruct(a.shape, a.dtype) for a in (weight, gate_t)]
        out_specs += [vectors, vectors]
        scratch.append(pltpu.SemaphoreType.DMA((2 + 2 * SPLIT,)))
    return pl.pallas_call(
        lambda *refs: project_kernel(other, *refs),
        in_specs=in_specs,
        out_specs=out_specs,
        out_shape=out_shape,
        scratch_shapes=scratch,
        input_output_aliases=aliases,
        cost_estimate=pl.CostEstimate(
            flops=4 * rows * depth * width,
            bytes_accessed=2 * weight.size + 8 * xs[0].size,
            transcendentals=0,
        ),
        compiler_params=pltpu.CompilerParams(vmem_limit_bytes=PROJECT_VMEM),
        name="project_other" if other else "project_own",
    )(*operands)


def base_inverses(lowers):
    count = CHUNK // BASE
    tiles = BASE // 8
    lane_block = iota((8, CHUNK), 1) // BASE
    inside = iota((8, CHUNK), 1) % BASE
    packed, results = [], []
    for lower in lowers:
        pack, result = [], []
        for t in range(tiles):
            tile = jnp.zeros((8, CHUNK), F32)
            for b in range(count):
                start = b * BASE + 8 * t
                tile = jnp.where(lane_block == b, lower[start : start + 8], tile)
            pack.append(tile)
            result.append(jnp.where(inside == iota((8, CHUNK), 0) + 8 * t, 1.0, 0.0))
        packed.append(pack)
        results.append(result)
    for j in range(BASE - 1):
        source = lane_block * BASE + j
        for pack, result in zip(packed, results):
            row = jnp.broadcast_to(result[j // 8][j % 8 : j % 8 + 1], (8, CHUNK))
            for t in range((j + 1) // 8, tiles):
                column = jnp.take_along_axis(pack[t], source, axis=1)
                result[t] = result[t] - column * row
    block = iota((BASE, CHUNK), 1) // BASE
    totals = []
    for result in results:
        side = jnp.concatenate(result, axis=0)
        totals.append(
            jnp.concatenate([jnp.where(block == b, side, 0.0) for b in range(count)], axis=0)
        )
    return totals


def inverses(lowers):
    totals = base_inverses(lowers)
    row, column = iota((CHUNK, CHUNK), 0), iota((CHUNK, CHUNK), 1)
    size = BASE
    while size < CHUNK:
        inside = (row // (2 * size) == column // (2 * size)) & (row // size > column // size)
        parts = [halves(total) for total in totals]
        corners = [halves(jnp.where(inside, lower, 0.0)) for lower in lowers]
        inner = [halves(dot3(c, p)) for c, p in zip(corners, parts)]
        totals = [t - dot3(p, i) for t, p, i in zip(totals, parts, inner)]
        size *= 2
    return totals


def activated(extended, slot, message, block, f, half, taps, first):
    rows = CHUNK
    lanes = slice(half * HEAD, (half + 1) * HEAD)
    rim = message[4 * block + f, rows:, lanes].astype(F32)
    before = message[4 * jnp.maximum(block - 1, 0) + f, rows - RIM : rows, lanes].astype(F32)
    extended[slot, :RIM] = jnp.where(block == 0, rim, before)
    extended[slot, RIM:] = message[4 * block + f, :rows, lanes].astype(F32)
    weights = taps[:, pl.ds(pl.multiple_of(first * HEAD, HEAD), HEAD)].astype(F32)
    total = jnp.zeros((rows, HEAD), F32)
    for tap in range(KERNEL):
        begin = RIM - (KERNEL - 1) + tap
        total = total + weights[tap : tap + 1] * extended[slot, begin : begin + rows]
    middle = 0.5 * total
    return middle + middle * jnp.tanh(middle)


def unit(vectors):
    return vectors * lax.rsqrt(jnp.sum(vectors * vectors, axis=-1, keepdims=True) + 1e-06)


def prepare_kernel(seg_product, place, rate, bias, taps, message, *rest):
    carry_out, add_out, high_out, low_out, ratio_out, growth_out, key_high, key_low = rest[:8]
    final = rest[8]
    if seg_product:
        product_out, extended, state, product = rest[9:]
    else:
        extended, state = rest[9:]
    j = place[0]
    rows = CHUNK
    blocks = carry_out.shape[0]

    row, column = iota((rows, rows), 0), iota((rows, rows), 1)
    strict, within = row > column, row >= column
    eye = jnp.where(row == column, 1.0, 0.0)
    upper = jnp.where(row <= column, 1.0, 0.0)
    lower_eye = jnp.concatenate([jnp.where(within, 1.0, 0.0), eye], axis=0)
    heads = [SPLIT * h + j for h in range(PAIR)]
    state[...] = jnp.zeros_like(state)
    if seg_product:
        product[...] = jnp.broadcast_to(eye, product.shape)

    def gate_tables(block):
        decay_rows, strength_rows = [], []
        for u in range(UNITS):
            h, a = u // 2, u % 2
            head = 2 * heads[h] + a
            lanes = slice(a * HEAD, (a + 1) * HEAD)

            def gate(f):
                parts = message[4 * block + f, rows : rows + EXTRA, lanes].astype(F32)
                return (parts[0:1] + parts[1:2]) + parts[2:3]

            strength_rows.append(1.0 / (1.0 + jnp.exp(-gate(h))))
            shift = gate(2 + h) + bias[head]
            soft = jnp.maximum(shift, 0.0) + jnp.log1p(jnp.exp(-jnp.abs(shift)))
            decay_rows.append(-rate[head] * soft)
        return jnp.concatenate(decay_rows + strength_rows, axis=0)

    def several(index, _):
        group = [GROUPED * index + i for i in range(GROUPED)]
        tables = jnp.concatenate([gate_tables(block) for block in group], axis=0)
        sums = jnp.dot(tables, upper, precision=HIGHEST, preferred_element_type=F32)
        turned = lax.dot_general(
            lower_eye, tables, (((1,), (1,)), ((), ())), precision=HIGHEST, preferred_element_type=F32
        )
        keys, keys_t, scores = [], [], []
        for i, block in enumerate(group):
            for h in range(PAIR):
                slot = (PAIR + UNITS) * i + h
                key = unit(activated(extended, slot, message, block, 1, h, taps, HK + heads[h]))
                keys.append(key)
                keys_t.append(key.T)
                parts = halves(keys_t[-1])
                key_high[block, h], key_low[block, h] = parts
                scores.append(dot3(halves(key), parts))
        growths, strengths, lasts, trailings, lowers = [], [], [], [], []
        for i, block in enumerate(group):
            growth_all = jnp.exp(turned[:rows, 2 * UNITS * i : 2 * UNITS * (i + 1)])
            growth_out[block] = growth_all
            for u in range(UNITS):
                at = 2 * UNITS * i + u
                cum_c = turned[:rows, at : at + 1]
                strength = turned[rows:, at + UNITS : at + UNITS + 1]
                cum_r = sums[at : at + 1]
                last = sums[at : at + 1, rows - 1 : rows]
                ratio = jnp.where(within, jnp.exp(jnp.minimum(cum_c - cum_r, 0.0)), 0.0)
                ratio_out[block, u] = ratio
                growths.append(growth_all[:, u : u + 1])
                strengths.append(strength)
                lasts.append(last)
                trailings.append(jnp.exp(jnp.minimum(last - cum_r, 0.0)))
                score = scores[PAIR * i + u // 2]
                lowers.append(jnp.where(strict, strength * ratio * score, 0.0))
        solves = inverses(lowers)
        weighted = []
        for i, block in enumerate(group):
            for u in range(UNITS):
                h, a, at = u // 2, u % 2, UNITS * i + u
                slot = (PAIR + UNITS) * i + PAIR + u
                first = 2 * HK + 2 * heads[h] + a
                value = activated(extended, slot, message, block, 2 + h, a, taps, first)
                scaled = jnp.concatenate(
                    [(strengths[at] * growths[at]) * keys[PAIR * i + h], strengths[at] * value],
                    axis=1,
                )
                weighted.append(halves(dot3(halves(solves[at]), halves(scaled))))
                high_out[block, u], low_out[block, u] = weighted[at]
        carries, adds = [], []
        for i, block in enumerate(group):
            for u in range(UNITS):
                at = UNITS * i + u
                left = trailings[at] * keys_t[PAIR * i + u // 2]
                mixed = dot3(halves(left), weighted[at])
                carry = jnp.exp(lasts[at]) * eye - mixed[:, :HEAD]
                carry_out[block, u] = carry
                add_out[block, u] = mixed[:, HEAD:]
                carries.append(halves(carry))
                adds.append(mixed[:, HEAD:])
        for i in range(GROUPED):
            for u in range(UNITS):
                at = UNITS * i + u
                state[u] = dot3(carries[at], halves(state[u])) + adds[at]
                if seg_product:
                    product[u] = dot3(carries[at], halves(product[u]))
        return 0

    lax.fori_loop(0, blocks // GROUPED, several, 0)
    final[...] = state[...].astype(final.dtype)
    if seg_product:
        product_out[...] = product[...].astype(product_out.dtype)


def prepare(place, rate, bias, message, taps, seg_product):
    blocks = message.shape[0] // 4
    rows = message.shape[1] - EXTRA
    assert rows == CHUNK
    state_shape = (UNITS, HEAD, HEAD)
    streams = [
        (state_shape, F32),
        (state_shape, F32),
        ((UNITS, rows, 2 * HEAD), BF16),
        ((UNITS, rows, 2 * HEAD), BF16),
        ((UNITS, rows, rows), F32),
        ((rows, 2 * UNITS), F32),
        ((PAIR, HEAD, rows), BF16),
        ((PAIR, HEAD, rows), BF16),
    ]
    out_shape = [jax.ShapeDtypeStruct((blocks,) + shape, dtype) for shape, dtype in streams]
    out_shape.append(jax.ShapeDtypeStruct(state_shape, BF16))
    scratch = [
        pltpu.VMEM(((PAIR + UNITS) * GROUPED, RIM + rows, HEAD), F32),
        pltpu.VMEM(state_shape, F32),
    ]
    if seg_product:
        out_shape.append(jax.ShapeDtypeStruct(state_shape, F32))
        scratch.append(pltpu.VMEM(state_shape, F32))
    scalars = pl.BlockSpec(memory_space=pltpu.SMEM)
    vectors = pl.BlockSpec(memory_space=pltpu.VMEM)
    return pl.pallas_call(
        lambda *refs: prepare_kernel(seg_product, *refs),
        in_specs=[scalars] * 3 + [vectors] * 2,
        out_specs=[vectors] * len(out_shape),
        out_shape=out_shape,
        scratch_shapes=scratch,
        compiler_params=pltpu.CompilerParams(vmem_limit_bytes=VMEM_LIMIT),
        name="prepare",
    )(place, rate, bias, taps, message)


def local_kernel(place, message, taps, high, low, ratio, growth, key_high, key_low, *rest):
    query_out, base_out, extended = rest
    heads = [SPLIT * h + place[0] for h in range(PAIR)]

    def one(block, _):
        queries, scores = [], []
        for h in range(PAIR):
            vectors = unit(activated(extended, h, message, block, 0, h, taps, heads[h]))
            queries.append(vectors * HEAD ** (-0.5))
            scores.append(dot3(halves(queries[h]), (key_high[block, h], key_low[block, h])))
        mixed = []
        for u in range(UNITS):
            mixing = ratio[block, u] * scores[u // 2]
            mixed.append(dot3(halves(mixing), (high[block, u], low[block, u])))
        for u in range(UNITS):
            query_out[block, u] = (
                growth[block, :, u : u + 1] * queries[u // 2] - mixed[u][:, :HEAD]
            )
            base_out[block, u] = mixed[u][:, HEAD:]
        return 0

    lax.fori_loop(0, query_out.shape[0], one, 0)


def local(place, message, taps, parts):
    blocks = message.shape[0] // 4
    rows = message.shape[1] - EXTRA
    shape = (blocks, UNITS, rows, HEAD)
    vectors = pl.BlockSpec(memory_space=pltpu.VMEM)
    flops = blocks * UNITS * 2 * 3 * rows * rows * 3 * HEAD
    return pl.pallas_call(
        local_kernel,
        in_specs=[pl.BlockSpec(memory_space=pltpu.SMEM)] + [vectors] * (2 + len(parts)),
        out_specs=[vectors, vectors],
        out_shape=[jax.ShapeDtypeStruct(shape, F32)] * 2,
        scratch_shapes=[pltpu.VMEM((PAIR, RIM + rows, HEAD), F32)],
        cost_estimate=pl.CostEstimate(
            flops=flops, bytes_accessed=12 << 20, transcendentals=message.size
        ),
        compiler_params=pltpu.CompilerParams(vmem_limit_bytes=VMEM_LIMIT),
        name="local",
    )(place, message, taps, *parts)


def read_kernel(place, carry, add, query, base, start, gain, *rest):
    outs, state = rest[:-1], rest[-1]
    state[...] = start[...].astype(F32)

    def one(block, _):
        results = []
        for u in range(UNITS):
            left = jnp.concatenate([carry[block, u], query[block, u]], axis=0)
            both = dot3(halves(left), halves(state[u]))
            state[u] = both[:HEAD] + add[block, u]
            reads = both[HEAD:] + base[block, u]
            mean = jnp.mean(reads * reads, axis=-1, keepdims=True)
            results.append((reads / jnp.sqrt(mean + 1e-06) * gain[...]).astype(BF16))
        slot = jnp.bitwise_xor(block, place[0])
        for k, out in enumerate(outs):

            @pl.when(slot == k)
            def _(out=out):
                for u in range(UNITS):
                    out[:, u * HEAD : (u + 1) * HEAD] = results[u]

        return 0

    lax.fori_loop(0, carry.shape[0], one, 0)


def read(place, carry, add, query, base, start, gain):
    blocks, _, rows, _ = query.shape
    vectors = pl.BlockSpec(memory_space=pltpu.VMEM)
    return pl.pallas_call(
        read_kernel,
        in_specs=[pl.BlockSpec(memory_space=pltpu.SMEM)] + [vectors] * 6,
        out_specs=[vectors] * blocks,
        out_shape=[jax.ShapeDtypeStruct((rows, UNITS * HEAD), BF16)] * blocks,
        scratch_shapes=[pltpu.VMEM(start.shape, F32)],
        compiler_params=pltpu.CompilerParams(vmem_limit_bytes=VMEM_LIMIT),
        name="read",
    )(place, carry, add, query, base, start, gain)


def assemble_kernel(place, *refs):
    out = refs[-1]
    width = 2 * HEAD
    for k, piece in enumerate(refs[:-1]):
        source = jnp.bitwise_xor(place[0], k)
        for h in range(PAIR):
            first = pl.multiple_of((h * SPLIT + source) * width, width)
            out[0, :, pl.ds(first, width)] = piece[:, h * width : (h + 1) * width]


def assemble(place, pieces):
    rows = pieces[0].shape[0]
    return pl.pallas_call(
        assemble_kernel,
        in_specs=[pl.BlockSpec(memory_space=pltpu.SMEM)]
        + [pl.BlockSpec(memory_space=pltpu.VMEM)] * len(pieces),
        out_specs=pl.BlockSpec(memory_space=pltpu.VMEM),
        out_shape=jax.ShapeDtypeStruct((1, rows, HV * HEAD), BF16),
        compiler_params=pltpu.CompilerParams(vmem_limit_bytes=VMEM_LIMIT),
        name="assemble",
    )(place, *pieces)


def messages_direct(tokens, qkv_weight, gate_weight, seq_count):
    me = lax.axis_index("fsdp")
    rim_rows = tokens[tokens.shape[0] - RIM :]
    far = swapped(tokens, "fsdp", 2)
    near = swapped(tokens, "fsdp", 1)
    rim_0 = shifted(rim_rows, ("seg", "sq"), [(i, i + 1) for i in range(seq_count - 1)])
    rim_1 = swapped(rim_0, "fsdp", 1)
    rim_2 = swapped(rim_0, "fsdp", 2)
    gate_t = gate_weight.T
    place = me.astype(jnp.int32)[None]
    message, weight, gate_t = project(
        place,
        (in_hbm(tokens), near),
        (rim_0, rim_1),
        in_hbm(gate_t),
        in_hbm(qkv_weight),
        None,
    )
    third = swapped(far, "fsdp", 1)
    rim_3 = swapped(rim_2, "fsdp", 1)
    message = project(place, (far, third), (rim_2, rim_3), gate_t, weight, message)[0]
    message = message.reshape((SPLIT * 4,) + message.shape[2:])
    return lax.all_to_all(message, ("sq", "fsdp"), 0, 0, tiled=True)


def messages_staged(tokens, qkv_weight, gate_weight, seq_count):
    length = tokens.shape[0]
    every = lax.all_gather(tokens, "fsdp", axis=0)
    mixed = jnp.einsum("ild,dc->ilc", every, qkv_weight, preferred_element_type=F32).astype(BF16)
    mixed = lax.all_to_all(mixed, "fsdp", 0, 2, tiled=True)[0]
    rim = shifted(
        mixed[length - RIM :], ("seg", "sq"), [(i, i + 1) for i in range(seq_count - 1)]
    )
    gates = jnp.dot(tokens, gate_weight, preferred_element_type=F32)
    high = lax.reduce_precision(gates, 8, 7)
    middle = lax.reduce_precision(gates - high, 8, 7)
    parts = jnp.stack([high, middle, (gates - high) - middle]).astype(BF16)
    parts = parts.reshape(3, length, 4, SPLIT, 2).transpose(3, 2, 0, 4, 1)
    parts = parts.reshape(SPLIT, 4, 3, 2 * length)

    def by_target(rows):
        count = rows.shape[0]
        query_key = rows[:, : 2 * HK * HEAD].reshape(count, 2, PAIR, SPLIT, HEAD)
        query_key = query_key.transpose(3, 1, 0, 2, 4).reshape(SPLIT, 2, count, 2 * HEAD)
        value = rows[:, 2 * HK * HEAD :].reshape(count, PAIR, SPLIT, 2 * HEAD)
        return jnp.concatenate([query_key, value.transpose(2, 1, 0, 3)], axis=1)

    rim = by_target(rim)[:, :, 3:]
    message = jnp.concatenate([by_target(mixed), parts, rim], axis=2)
    message = lax.all_to_all(message, "sq", 0, 0, tiled=True)
    return message.reshape((SPLIT * 4,) + message.shape[2:])


def layer(inputs, qkv_weight, gate_weight, conv_weight, head_rate, dt_bias, norm_gain):
    segments = lax.axis_size("seg")
    tokens = inputs[0]
    build = messages_direct if lax.axis_size("fsdp") == 4 else messages_staged
    message = build(tokens, qkv_weight, gate_weight, segments * SPLIT)
    place = lax.axis_index("sq").astype(jnp.int32)[None]
    outs = prepare(place, head_rate, dt_bias, message, conv_weight, segments > 2)
    carry, add, parts, final = outs[0], outs[1], outs[2:8], outs[8]
    onward = [(i, i + 1) for i in range(segments - 1)]
    start = jnp.zeros_like(final)
    if segments == 2:
        start = shifted(final, "seg", onward)
    elif segments > 2:
        for _ in range(segments - 1):
            ahead = jnp.einsum("hij,hjk->hik", outs[9], start.astype(F32), precision=HIGHEST)
            start = shifted((ahead + final.astype(F32)).astype(BF16), "seg", onward)
    query, base = local(place, message, conv_weight, parts)
    pieces = read(place, carry, add, query, base, start, norm_gain[None])
    received = [pieces[0]] + [swapped(pieces[k], "sq", k) for k in range(1, SPLIT)]
    return assemble(place, received)


def solution(mesh):
    seq, fsdp = mesh.shape["seq"], mesh.shape["fsdp"]
    parts = Mesh(mesh.devices.reshape(seq // SPLIT, SPLIT, fsdp), ("seg", "sq", "fsdp"))
    split = P("fsdp", ("seg", "sq"), None)
    in_specs = (split, P(None, "fsdp"), P(), P(), P(), P(), P())
    return jax.shard_map(layer, mesh=parts, in_specs=in_specs, out_specs=split, check_vma=False)
```

```python
import jax
import jax.numpy as jnp
from jax import lax
from jax.experimental import pallas as pl
from jax.experimental.pallas import tpu as pltpu
from jax.sharding import Mesh
from jax.sharding import PartitionSpec as P


HEAD = 128
HK = 8
HV = 16
KERNEL = 4
PAIR = 2
SPLIT = HK // PAIR
CHUNK = 128
BASE = 16
PROJECT_VMEM = 24 << 20
VMEM_LIMIT = 24 << 20
GROUPED = 4
EXTRA = 8
RIM = 8
UNITS = HV // SPLIT
F32 = jnp.float32
BF16 = jnp.bfloat16
HIGHEST = lax.Precision.HIGHEST


def shifted(value, axes, pairs):
    return lax.ppermute(value, axes, pairs)


def swapped(value, axis, bit):
    count = lax.axis_size(axis)
    return lax.ppermute(value, axis, [(i, i ^ bit) for i in range(count)])


def in_hbm(value):
    return pltpu.with_memory_space_constraint(value, pltpu.HBM)


def dot(a, b):
    return jnp.dot(a, b, preferred_element_type=F32)


def halves(a):
    high = a.astype(BF16)
    return high, (a - high.astype(F32)).astype(BF16)


def dot3(a, b):
    right = jnp.concatenate([jnp.concatenate(b, axis=1), jnp.concatenate([b[0], jnp.zeros_like(b[0])], axis=1)], axis=0)
    both = dot(jnp.concatenate(a, axis=1), right)
    width = b[0].shape[1]
    return both[:, :width] + both[:, width:]


def split3(a):
    high = a.astype(BF16).astype(F32)
    rest = a - high
    middle = rest.astype(BF16).astype(F32)
    return high, middle, rest - middle


def iota(shape, dim):
    return lax.broadcasted_iota(jnp.int32, shape, dim)


def project_kernel(other, place, x0, x1, rim_0, rim_1, gate_hbm, weight_hbm, *rest):
    rows = x0.shape[0]
    me = place[0]
    pair = 1 - me // 2 if other else me // 2
    contiguous = me >= 2
    loads = []

    def lane(j, a):
        return pl.multiple_of(jnp.where(contiguous, 2 * j + a, SPLIT * a + j) * HEAD, HEAD)

    def load(source, target, sem):
        copy = pltpu.make_async_copy(source, target, sem)
        copy.start()
        loads.append(copy)

    if other:
        out, lhs, stage, gates, sems = rest[-5:]
        weight, gate_t = weight_hbm, gate_hbm
        lhs[:rows, :] = x0[...]
    else:
        out, weight, gate_t, lhs, stage, gates, sems, load_sems = rest
        load(x0, lhs.at[pl.ds(0, rows)], load_sems.at[0])
        load(gate_hbm, gate_t, load_sems.at[1])
        for j in range(SPLIT):
            for a in range(2):
                part = pl.ds(lane(j, a), HEAD)
                load(weight_hbm.at[:, part], weight.at[:, part], load_sems.at[2 + 2 * j + a])
    lhs[rows : 2 * rows, :] = x1[...]
    lhs[2 * rows :, :] = jnp.concatenate([rim_0[...], rim_1[...]], axis=0)
    for copy in loads[:2]:
        copy.wait()
    gates[...] = lax.dot_general(
        gate_t[...], lhs[: 2 * rows, :], (((1,), (1,)), ((), ())), preferred_element_type=F32
    )
    share = gate_t.shape[0] // 4
    parts = split3(gates[pl.ds(pl.multiple_of(me * share, share), share), :])
    index = iota((RIM, 2 * HEAD), 0)
    copies = []
    for j in range(SPLIT):
        for copy in loads[2 + 2 * j : 4 + 2 * j]:
            copy.wait()
        columns = jnp.concatenate([weight[:, pl.ds(lane(j, a), HEAD)] for a in range(2)], axis=1)
        mixed = dot(lhs[...], columns)
        for k in range(2):
            target = jnp.bitwise_xor(me % 2, k)
            stage[j, target, :rows, :] = mixed[k * rows : (k + 1) * rows].astype(BF16)
            tokens = slice(k * rows, (k + 1) * rows)
            tail = mixed[2 * rows + k * RIM : 2 * rows + (k + 1) * RIM]
            for part in range(3):
                gate = [parts[part][2 * j + a : 2 * j + a + 1, tokens] for a in range(2)]
                tail = jnp.where(index == part, jnp.concatenate(gate, axis=1), tail)
            stage[j, target, rows:, :] = tail.astype(BF16)
        copy = pltpu.make_async_copy(stage.at[j], out.at[j, pl.ds(2 * pair, 2)], sems.at[j])
        copy.start()
        copies.append(copy)
    for copy in copies:
        copy.wait()


def project(place, xs, rims, gate_t, weight, message):
    other = message is not None
    rows, depth = xs[0].shape
    width = weight.shape[1]
    vectors, anywhere = pl.BlockSpec(memory_space=pltpu.VMEM), pl.BlockSpec(memory_space=pl.ANY)
    operands = [place, *xs, *rims, gate_t, weight]
    first = vectors if other else pl.BlockSpec(memory_space=pltpu.HBM)
    in_specs = [pl.BlockSpec(memory_space=pltpu.SMEM), first] + [vectors] * 3 + [first] * 2
    message_shape = (SPLIT, 4, rows + EXTRA, 2 * HEAD)
    out_shape = [jax.ShapeDtypeStruct(message_shape, BF16)]
    out_specs = [anywhere]
    scratch = [
        pltpu.VMEM((2 * rows + 2 * RIM, depth), BF16),
        pltpu.VMEM((SPLIT, 2, rows + EXTRA, 2 * HEAD), BF16),
        pltpu.VMEM((gate_t.shape[0], 2 * rows), F32),
        pltpu.SemaphoreType.DMA((SPLIT,)),
    ]
    aliases = {}
    if other:
        aliases = {len(operands): 0}
        operands.append(message)
        in_specs.append(anywhere)
    else:
        out_shape += [jax.ShapeDtypeStruct(a.shape, a.dtype) for a in (weight, gate_t)]
        out_specs += [vectors, vectors]
        scratch.append(pltpu.SemaphoreType.DMA((2 + 2 * SPLIT,)))
    return pl.pallas_call(
        lambda *refs: project_kernel(other, *refs),
        in_specs=in_specs,
        out_specs=out_specs,
        out_shape=out_shape,
        scratch_shapes=scratch,
        input_output_aliases=aliases,
        cost_estimate=pl.CostEstimate(
            flops=4 * rows * depth * width,
            bytes_accessed=2 * weight.size + 8 * xs[0].size,
            transcendentals=0,
        ),
        compiler_params=pltpu.CompilerParams(vmem_limit_bytes=PROJECT_VMEM),
        name="project_other" if other else "project_own",
    )(*operands)


def base_inverses(lowers):
    count = CHUNK // BASE
    tiles = BASE // 8
    lane_block = iota((8, CHUNK), 1) // BASE
    inside = iota((8, CHUNK), 1) % BASE
    packed, results = [], []
    for lower in lowers:
        pack, result = [], []
        for t in range(tiles):
            tile = jnp.zeros((8, CHUNK), F32)
            for b in range(count):
                start = b * BASE + 8 * t
                tile = jnp.where(lane_block == b, lower[start : start + 8], tile)
            pack.append(tile)
            result.append(jnp.where(inside == iota((8, CHUNK), 0) + 8 * t, 1.0, 0.0))
        packed.append(pack)
        results.append(result)
    for j in range(BASE - 1):
        source = lane_block * BASE + j
        for pack, result in zip(packed, results):
            row = jnp.broadcast_to(result[j // 8][j % 8 : j % 8 + 1], (8, CHUNK))
            for t in range((j + 1) // 8, tiles):
                column = jnp.take_along_axis(pack[t], source, axis=1)
                result[t] = result[t] - column * row
    block = iota((BASE, CHUNK), 1) // BASE
    totals = []
    for result in results:
        side = jnp.concatenate(result, axis=0)
        totals.append(
            jnp.concatenate([jnp.where(block == b, side, 0.0) for b in range(count)], axis=0)
        )
    return totals


def odd_blocks(value, size):
    return jnp.concatenate([value[r : r + size] for r in range(size, CHUNK, 2 * size)], axis=0)


def between(even, odd, size):
    blocks = []
    for r in range(0, CHUNK // 2, size):
        blocks += [even[r : r + size], odd[r : r + size]]
    return jnp.concatenate(blocks, axis=0)


def inverses(lowers):
    totals = base_inverses(lowers)
    row, column = iota((CHUNK // 2, CHUNK), 0), iota((CHUNK // 2, CHUNK), 1)
    blank = jnp.zeros((CHUNK // 2, CHUNK), BF16)
    size = BASE
    while size < CHUNK:
        inside = column // size == 2 * (row // size)
        parts = [halves(total) for total in totals]
        corners = [halves(jnp.where(inside, odd_blocks(lower, size), 0.0)) for lower in lowers]
        inner = [halves(dot3(c, p)) for c, p in zip(corners, parts)]
        for i, total in enumerate(totals):
            left = [odd_blocks(part, size) for part in parts[i]]
            right = [between(blank, part, size) for part in inner[i]]
            odd = odd_blocks(total, size) - dot3(left, right)
            even = jnp.concatenate([total[r : r + size] for r in range(0, CHUNK, 2 * size)], axis=0)
            totals[i] = between(even, odd, size)
        size *= 2
    return totals


def activated(extended, slot, message, block, f, half, taps, first):
    rows = CHUNK
    lanes = slice(half * HEAD, (half + 1) * HEAD)
    rim = message[4 * block + f, rows:, lanes].astype(F32)
    before = message[4 * jnp.maximum(block - 1, 0) + f, rows - RIM : rows, lanes].astype(F32)
    extended[slot, :RIM] = jnp.where(block == 0, rim, before)
    extended[slot, RIM:] = message[4 * block + f, :rows, lanes].astype(F32)
    weights = taps[:, pl.ds(pl.multiple_of(first * HEAD, HEAD), HEAD)].astype(F32)
    total = jnp.zeros((rows, HEAD), F32)
    for tap in range(KERNEL):
        begin = RIM - (KERNEL - 1) + tap
        total = total + weights[tap : tap + 1] * extended[slot, begin : begin + rows]
    middle = 0.5 * total
    return middle + middle * jnp.tanh(middle)


def unit(vectors):
    return vectors * lax.rsqrt(jnp.sum(vectors * vectors, axis=-1, keepdims=True) + 1e-06)


def prepare_kernel(seg_product, place, rate, bias, taps, message, *rest):
    carry_out, add_out, high_out, low_out, ratio_out, growth_out, key_high, key_low = rest[:8]
    final = rest[8]
    if seg_product:
        product_out, extended, state, product = rest[9:]
    else:
        extended, state = rest[9:]
    j = place[0]
    rows = CHUNK
    blocks = carry_out.shape[0]

    row, column = iota((rows, rows), 0), iota((rows, rows), 1)
    strict, within = row > column, row >= column
    eye = jnp.where(row == column, 1.0, 0.0)
    upper = jnp.where(row <= column, 1.0, 0.0)
    lower_eye = jnp.concatenate([jnp.where(within, 1.0, 0.0), eye], axis=0)
    heads = [SPLIT * h + j for h in range(PAIR)]
    state[...] = jnp.zeros_like(state)
    if seg_product:
        product[...] = jnp.broadcast_to(eye, product.shape)

    def gate_tables(block):
        decay_rows, strength_rows = [], []
        for u in range(UNITS):
            h, a = u // 2, u % 2
            head = 2 * heads[h] + a
            lanes = slice(a * HEAD, (a + 1) * HEAD)

            def gate(f):
                parts = message[4 * block + f, rows : rows + EXTRA, lanes].astype(F32)
                return (parts[0:1] + parts[1:2]) + parts[2:3]

            strength_rows.append(1.0 / (1.0 + jnp.exp(-gate(h))))
            shift = gate(2 + h) + bias[head]
            soft = jnp.maximum(shift, 0.0) + jnp.log1p(jnp.exp(-jnp.abs(shift)))
            decay_rows.append(-rate[head] * soft)
        return jnp.concatenate(decay_rows + strength_rows, axis=0)

    def several(index, _):
        group = [GROUPED * index + i for i in range(GROUPED)]
        tables = jnp.concatenate([gate_tables(block) for block in group], axis=0)
        sums = jnp.dot(tables, upper, precision=HIGHEST, preferred_element_type=F32)
        turned = lax.dot_general(
            lower_eye, tables, (((1,), (1,)), ((), ())), precision=HIGHEST, preferred_element_type=F32
        )
        keys, keys_t, scores = [], [], []
        for i, block in enumerate(group):
            for h in range(PAIR):
                slot = (PAIR + UNITS) * i + h
                key = unit(activated(extended, slot, message, block, 1, h, taps, HK + heads[h]))
                keys.append(key)
                keys_t.append(key.T)
                parts = halves(keys_t[-1])
                key_high[block, h], key_low[block, h] = parts
                scores.append(dot3(halves(key), parts))
        growths, strengths, lasts, trailings, lowers = [], [], [], [], []
        for i, block in enumerate(group):
            growth_all = jnp.exp(turned[:rows, 2 * UNITS * i : 2 * UNITS * (i + 1)])
            growth_out[block] = growth_all
            for u in range(UNITS):
                at = 2 * UNITS * i + u
                cum_c = turned[:rows, at : at + 1]
                strength = turned[rows:, at + UNITS : at + UNITS + 1]
                cum_r = sums[at : at + 1]
                last = sums[at : at + 1, rows - 1 : rows]
                ratio = jnp.where(within, jnp.exp(jnp.minimum(cum_c - cum_r, 0.0)), 0.0)
                ratio_out[block, u] = ratio
                growths.append(growth_all[:, u : u + 1])
                strengths.append(strength)
                lasts.append(last)
                trailings.append(jnp.exp(jnp.minimum(last - cum_r, 0.0)))
                score = scores[PAIR * i + u // 2]
                lowers.append(jnp.where(strict, strength * ratio * score, 0.0))
        solves = inverses(lowers)
        weighted = []
        for i, block in enumerate(group):
            for u in range(UNITS):
                h, a, at = u // 2, u % 2, UNITS * i + u
                slot = (PAIR + UNITS) * i + PAIR + u
                first = 2 * HK + 2 * heads[h] + a
                value = activated(extended, slot, message, block, 2 + h, a, taps, first)
                scaled = jnp.concatenate(
                    [(strengths[at] * growths[at]) * keys[PAIR * i + h], strengths[at] * value],
                    axis=1,
                )
                weighted.append(halves(dot3(halves(solves[at]), halves(scaled))))
                high_out[block, u], low_out[block, u] = weighted[at]
        carries, adds = [], []
        for i, block in enumerate(group):
            for u in range(UNITS):
                at = UNITS * i + u
                left = trailings[at] * keys_t[PAIR * i + u // 2]
                mixed = dot3(halves(left), weighted[at])
                carry = jnp.exp(lasts[at]) * eye - mixed[:, :HEAD]
                carry_out[block, u] = carry
                add_out[block, u] = mixed[:, HEAD:]
                carries.append(halves(carry))
                adds.append(mixed[:, HEAD:])
        for i in range(GROUPED):
            for u in range(UNITS):
                at = UNITS * i + u
                state[u] = dot3(carries[at], halves(state[u])) + adds[at]
                if seg_product:
                    product[u] = dot3(carries[at], halves(product[u]))
        return 0

    lax.fori_loop(0, blocks // GROUPED, several, 0)
    final[...] = state[...].astype(final.dtype)
    if seg_product:
        product_out[...] = product[...].astype(product_out.dtype)


def prepare(place, rate, bias, message, taps, seg_product):
    blocks = message.shape[0] // 4
    rows = message.shape[1] - EXTRA
    assert rows == CHUNK
    state_shape = (UNITS, HEAD, HEAD)
    streams = [
        (state_shape, F32),
        (state_shape, F32),
        ((UNITS, rows, 2 * HEAD), BF16),
        ((UNITS, rows, 2 * HEAD), BF16),
        ((UNITS, rows, rows), F32),
        ((rows, 2 * UNITS), F32),
        ((PAIR, HEAD, rows), BF16),
        ((PAIR, HEAD, rows), BF16),
    ]
    out_shape = [jax.ShapeDtypeStruct((blocks,) + shape, dtype) for shape, dtype in streams]
    out_shape.append(jax.ShapeDtypeStruct(state_shape, BF16))
    scratch = [
        pltpu.VMEM(((PAIR + UNITS) * GROUPED, RIM + rows, HEAD), F32),
        pltpu.VMEM(state_shape, F32),
    ]
    if seg_product:
        out_shape.append(jax.ShapeDtypeStruct(state_shape, F32))
        scratch.append(pltpu.VMEM(state_shape, F32))
    scalars = pl.BlockSpec(memory_space=pltpu.SMEM)
    vectors = pl.BlockSpec(memory_space=pltpu.VMEM)
    return pl.pallas_call(
        lambda *refs: prepare_kernel(seg_product, *refs),
        in_specs=[scalars] * 3 + [vectors] * 2,
        out_specs=[vectors] * len(out_shape),
        out_shape=out_shape,
        scratch_shapes=scratch,
        compiler_params=pltpu.CompilerParams(vmem_limit_bytes=VMEM_LIMIT),
        name="prepare",
    )(place, rate, bias, taps, message)


def local_kernel(place, message, taps, high, low, ratio, growth, key_high, key_low, *rest):
    query_out, base_out, extended = rest
    heads = [SPLIT * h + place[0] for h in range(PAIR)]

    def one(block, _):
        queries, scores = [], []
        for h in range(PAIR):
            vectors = unit(activated(extended, h, message, block, 0, h, taps, heads[h]))
            queries.append(vectors * HEAD ** (-0.5))
            scores.append(dot3(halves(queries[h]), (key_high[block, h], key_low[block, h])))
        mixed = []
        for u in range(UNITS):
            mixing = ratio[block, u] * scores[u // 2]
            mixed.append(dot3(halves(mixing), (high[block, u], low[block, u])))
        for u in range(UNITS):
            query_out[block, u] = (
                growth[block, :, u : u + 1] * queries[u // 2] - mixed[u][:, :HEAD]
            )
            base_out[block, u] = mixed[u][:, HEAD:]
        return 0

    lax.fori_loop(0, query_out.shape[0], one, 0)


def local(place, message, taps, parts):
    blocks = message.shape[0] // 4
    rows = message.shape[1] - EXTRA
    shape = (blocks, UNITS, rows, HEAD)
    vectors = pl.BlockSpec(memory_space=pltpu.VMEM)
    flops = blocks * UNITS * 2 * 3 * rows * rows * 3 * HEAD
    return pl.pallas_call(
        local_kernel,
        in_specs=[pl.BlockSpec(memory_space=pltpu.SMEM)] + [vectors] * (2 + len(parts)),
        out_specs=[vectors, vectors],
        out_shape=[jax.ShapeDtypeStruct(shape, F32)] * 2,
        scratch_shapes=[pltpu.VMEM((PAIR, RIM + rows, HEAD), F32)],
        cost_estimate=pl.CostEstimate(
            flops=flops, bytes_accessed=12 << 20, transcendentals=message.size
        ),
        compiler_params=pltpu.CompilerParams(vmem_limit_bytes=VMEM_LIMIT),
        name="local",
    )(place, message, taps, *parts)


def read_kernel(place, carry, add, query, base, start, gain, *rest):
    outs, (stage, state) = rest[:-2], rest[-2:]
    state[...] = start[...].astype(F32)
    for block in range(carry.shape[0]):
        slot = jnp.bitwise_xor(block, place[0])
        for u in range(UNITS):
            left = jnp.concatenate([carry[block, u], query[block, u]], axis=0)
            both = dot3(halves(left), halves(state[u]))
            state[u] = both[:HEAD] + add[block, u]
            reads = both[HEAD:] + base[block, u]
            mean = jnp.mean(reads * reads, axis=-1, keepdims=True)
            stage[slot, :, u * HEAD : (u + 1) * HEAD] = (
                reads / jnp.sqrt(mean + 1e-06) * gain[...]
            ).astype(BF16)
    for k, out in enumerate(outs):
        out[...] = stage[k]


def read(place, carry, add, query, base, start, gain):
    blocks, _, rows, _ = query.shape
    vectors = pl.BlockSpec(memory_space=pltpu.VMEM)
    return pl.pallas_call(
        read_kernel,
        in_specs=[pl.BlockSpec(memory_space=pltpu.SMEM)] + [vectors] * 6,
        out_specs=[vectors] * blocks,
        out_shape=[jax.ShapeDtypeStruct((rows, UNITS * HEAD), BF16)] * blocks,
        scratch_shapes=[
            pltpu.VMEM((blocks, rows, UNITS * HEAD), BF16),
            pltpu.VMEM(start.shape, F32),
        ],
        compiler_params=pltpu.CompilerParams(vmem_limit_bytes=VMEM_LIMIT),
        name="read",
    )(place, carry, add, query, base, start, gain)


def assemble_kernel(place, *refs):
    out = refs[-1]
    width = 2 * HEAD
    for k, piece in enumerate(refs[:-1]):
        source = jnp.bitwise_xor(place[0], k)
        for h in range(PAIR):
            first = pl.multiple_of((h * SPLIT + source) * width, width)
            out[0, :, pl.ds(first, width)] = piece[:, h * width : (h + 1) * width]


def assemble(place, pieces):
    rows = pieces[0].shape[0]
    return pl.pallas_call(
        assemble_kernel,
        in_specs=[pl.BlockSpec(memory_space=pltpu.SMEM)]
        + [pl.BlockSpec(memory_space=pltpu.VMEM)] * len(pieces),
        out_specs=pl.BlockSpec(memory_space=pltpu.VMEM),
        out_shape=jax.ShapeDtypeStruct((1, rows, HV * HEAD), BF16),
        compiler_params=pltpu.CompilerParams(vmem_limit_bytes=VMEM_LIMIT),
        name="assemble",
    )(place, *pieces)


def messages_direct(tokens, qkv_weight, gate_weight, seq_count):
    me = lax.axis_index("fsdp")
    rim_rows = tokens[tokens.shape[0] - RIM :]
    far = swapped(tokens, "fsdp", 2)
    near = swapped(tokens, "fsdp", 1)
    rim_0 = shifted(rim_rows, ("seg", "sq"), [(i, i + 1) for i in range(seq_count - 1)])
    rim_1 = swapped(rim_0, "fsdp", 1)
    rim_2 = swapped(rim_0, "fsdp", 2)
    gate_t = gate_weight.T
    place = me.astype(jnp.int32)[None]
    message, weight, gate_t = project(
        place,
        (in_hbm(tokens), near),
        (rim_0, rim_1),
        in_hbm(gate_t),
        in_hbm(qkv_weight),
        None,
    )
    third = swapped(far, "fsdp", 1)
    rim_3 = swapped(rim_2, "fsdp", 1)
    message = project(place, (far, third), (rim_2, rim_3), gate_t, weight, message)[0]
    message = message.reshape((SPLIT * 4,) + message.shape[2:])
    return lax.all_to_all(message, ("sq", "fsdp"), 0, 0, tiled=True)


def messages_staged(tokens, qkv_weight, gate_weight, seq_count):
    length = tokens.shape[0]
    every = lax.all_gather(tokens, "fsdp", axis=0)
    mixed = jnp.einsum("ild,dc->ilc", every, qkv_weight, preferred_element_type=F32).astype(BF16)
    mixed = lax.all_to_all(mixed, "fsdp", 0, 2, tiled=True)[0]
    rim = shifted(
        mixed[length - RIM :], ("seg", "sq"), [(i, i + 1) for i in range(seq_count - 1)]
    )
    gates = jnp.dot(tokens, gate_weight, preferred_element_type=F32)
    high = lax.reduce_precision(gates, 8, 7)
    middle = lax.reduce_precision(gates - high, 8, 7)
    parts = jnp.stack([high, middle, (gates - high) - middle]).astype(BF16)
    parts = parts.reshape(3, length, 4, SPLIT, 2).transpose(3, 2, 0, 4, 1)
    parts = parts.reshape(SPLIT, 4, 3, 2 * length)

    def by_target(rows):
        count = rows.shape[0]
        query_key = rows[:, : 2 * HK * HEAD].reshape(count, 2, PAIR, SPLIT, HEAD)
        query_key = query_key.transpose(3, 1, 0, 2, 4).reshape(SPLIT, 2, count, 2 * HEAD)
        value = rows[:, 2 * HK * HEAD :].reshape(count, PAIR, SPLIT, 2 * HEAD)
        return jnp.concatenate([query_key, value.transpose(2, 1, 0, 3)], axis=1)

    rim = by_target(rim)[:, :, 3:]
    message = jnp.concatenate([by_target(mixed), parts, rim], axis=2)
    message = lax.all_to_all(message, "sq", 0, 0, tiled=True)
    return message.reshape((SPLIT * 4,) + message.shape[2:])


def layer(inputs, qkv_weight, gate_weight, conv_weight, head_rate, dt_bias, norm_gain):
    segments = lax.axis_size("seg")
    tokens = inputs[0]
    build = messages_direct if lax.axis_size("fsdp") == 4 else messages_staged
    message = build(tokens, qkv_weight, gate_weight, segments * SPLIT)
    place = lax.axis_index("sq").astype(jnp.int32)[None]
    outs = prepare(place, head_rate, dt_bias, message, conv_weight, segments > 2)
    carry, add, parts, final = outs[0], outs[1], outs[2:8], outs[8]
    onward = [(i, i + 1) for i in range(segments - 1)]
    start = jnp.zeros_like(final)
    if segments == 2:
        start = shifted(final, "seg", onward)
    elif segments > 2:
        for _ in range(segments - 1):
            ahead = jnp.einsum("hij,hjk->hik", outs[9], start.astype(F32), precision=HIGHEST)
            start = shifted((ahead + final.astype(F32)).astype(BF16), "seg", onward)
    query, base = local(place, message, conv_weight, parts)
    pieces = read(place, carry, add, query, base, start, norm_gain[None])
    received = [pieces[0]] + [swapped(pieces[k], "sq", k) for k in range(1, SPLIT)]
    return assemble(place, received)


def solution(mesh):
    seq, fsdp = mesh.shape["seq"], mesh.shape["fsdp"]
    parts = Mesh(mesh.devices.reshape(seq // SPLIT, SPLIT, fsdp), ("seg", "sq", "fsdp"))
    split = P("fsdp", ("seg", "sq"), None)
    in_specs = (split, P(None, "fsdp"), P(), P(), P(), P(), P())
    return jax.shard_map(layer, mesh=parts, in_specs=in_specs, out_specs=split, check_vma=False)
```

```python
import jax
import jax.numpy as jnp
from jax import lax
from jax.experimental import pallas as pl
from jax.experimental.pallas import tpu as pltpu
from jax.sharding import Mesh
from jax.sharding import PartitionSpec as P


HEAD = 128
HK = 8
HV = 16
KERNEL = 4
PAIR = 2
SPLIT = HK // PAIR
CHUNK = 128
BASE = 16
PROJECT_VMEM = 24 << 20
VMEM_LIMIT = 24 << 20
GROUPED = 4
EXTRA = 8
RIM = 8
UNITS = HV // SPLIT
F32 = jnp.float32
BF16 = jnp.bfloat16
HIGHEST = lax.Precision.HIGHEST


def shifted(value, axes, pairs):
    return lax.ppermute(value, axes, pairs)


def swapped(value, axis, bit):
    count = lax.axis_size(axis)
    return lax.ppermute(value, axis, [(i, i ^ bit) for i in range(count)])


def in_hbm(value):
    return pltpu.with_memory_space_constraint(value, pltpu.HBM)


def dot(a, b):
    return jnp.dot(a, b, preferred_element_type=F32)


def halves(a):
    high = a.astype(BF16)
    return high, (a - high.astype(F32)).astype(BF16)


def dot3(a, b):
    right = jnp.concatenate([jnp.concatenate(b, axis=1), jnp.concatenate([b[0], jnp.zeros_like(b[0])], axis=1)], axis=0)
    both = dot(jnp.concatenate(a, axis=1), right)
    width = b[0].shape[1]
    return both[:, :width] + both[:, width:]


def dot3_stacked(a, b):
    rows, width = a[0].shape[0], b[0].shape[1]
    both = dot(jnp.concatenate(a, axis=0), jnp.concatenate(b, axis=1))
    return both[:rows, :width] + (both[:rows, width:] + both[rows:, :width])


def split3(a):
    high = a.astype(BF16).astype(F32)
    rest = a - high
    middle = rest.astype(BF16).astype(F32)
    return high, middle, rest - middle


def iota(shape, dim):
    return lax.broadcasted_iota(jnp.int32, shape, dim)


def project_kernel(other, place, x0, x1, rim_0, rim_1, gate_hbm, weight_hbm, *rest):
    rows = x0.shape[0]
    me = place[0]
    pair = 1 - me // 2 if other else me // 2
    contiguous = me >= 2
    loads = []

    def lane(j, a):
        return pl.multiple_of(jnp.where(contiguous, 2 * j + a, SPLIT * a + j) * HEAD, HEAD)

    def load(source, target, sem):
        copy = pltpu.make_async_copy(source, target, sem)
        copy.start()
        loads.append(copy)

    if other:
        out, lhs, stage, gates, sems = rest[-5:]
        weight, gate_t = weight_hbm, gate_hbm
        lhs[:rows, :] = x0[...]
    else:
        out, weight, gate_t, lhs, stage, gates, sems, load_sems = rest
        load(x0, lhs.at[pl.ds(0, rows)], load_sems.at[0])
        load(gate_hbm, gate_t, load_sems.at[1])
        for j in range(SPLIT):
            for a in range(2):
                part = pl.ds(lane(j, a), HEAD)
                load(weight_hbm.at[:, part], weight.at[:, part], load_sems.at[2 + 2 * j + a])
    lhs[rows : 2 * rows, :] = x1[...]
    lhs[2 * rows :, :] = jnp.concatenate([rim_0[...], rim_1[...]], axis=0)
    for copy in loads[:2]:
        copy.wait()
    gates[...] = lax.dot_general(
        gate_t[...], lhs[: 2 * rows, :], (((1,), (1,)), ((), ())), preferred_element_type=F32
    )
    share = gate_t.shape[0] // 4
    parts = split3(gates[pl.ds(pl.multiple_of(me * share, share), share), :])
    index = iota((RIM, 2 * HEAD), 0)
    copies = []
    for j in range(SPLIT):
        for copy in loads[2 + 2 * j : 4 + 2 * j]:
            copy.wait()
        columns = jnp.concatenate([weight[:, pl.ds(lane(j, a), HEAD)] for a in range(2)], axis=1)
        mixed = dot(lhs[...], columns)
        for k in range(2):
            target = jnp.bitwise_xor(me % 2, k)
            stage[j, target, :rows, :] = mixed[k * rows : (k + 1) * rows].astype(BF16)
            tokens = slice(k * rows, (k + 1) * rows)
            tail = mixed[2 * rows + k * RIM : 2 * rows + (k + 1) * RIM]
            for part in range(3):
                gate = [parts[part][2 * j + a : 2 * j + a + 1, tokens] for a in range(2)]
                tail = jnp.where(index == part, jnp.concatenate(gate, axis=1), tail)
            stage[j, target, rows:, :] = tail.astype(BF16)
        copy = pltpu.make_async_copy(stage.at[j], out.at[j, pl.ds(2 * pair, 2)], sems.at[j])
        copy.start()
        copies.append(copy)
    for copy in copies:
        copy.wait()


def project(place, xs, rims, gate_t, weight, message):
    other = message is not None
    rows, depth = xs[0].shape
    width = weight.shape[1]
    vectors, anywhere = pl.BlockSpec(memory_space=pltpu.VMEM), pl.BlockSpec(memory_space=pl.ANY)
    operands = [place, *xs, *rims, gate_t, weight]
    first = vectors if other else pl.BlockSpec(memory_space=pltpu.HBM)
    in_specs = [pl.BlockSpec(memory_space=pltpu.SMEM), first] + [vectors] * 3 + [first] * 2
    message_shape = (SPLIT, 4, rows + EXTRA, 2 * HEAD)
    out_shape = [jax.ShapeDtypeStruct(message_shape, BF16)]
    out_specs = [anywhere]
    scratch = [
        pltpu.VMEM((2 * rows + 2 * RIM, depth), BF16),
        pltpu.VMEM((SPLIT, 2, rows + EXTRA, 2 * HEAD), BF16),
        pltpu.VMEM((gate_t.shape[0], 2 * rows), F32),
        pltpu.SemaphoreType.DMA((SPLIT,)),
    ]
    aliases = {}
    if other:
        aliases = {len(operands): 0}
        operands.append(message)
        in_specs.append(anywhere)
    else:
        out_shape += [jax.ShapeDtypeStruct(a.shape, a.dtype) for a in (weight, gate_t)]
        out_specs += [vectors, vectors]
        scratch.append(pltpu.SemaphoreType.DMA((2 + 2 * SPLIT,)))
    return pl.pallas_call(
        lambda *refs: project_kernel(other, *refs),
        in_specs=in_specs,
        out_specs=out_specs,
        out_shape=out_shape,
        scratch_shapes=scratch,
        input_output_aliases=aliases,
        cost_estimate=pl.CostEstimate(
            flops=4 * rows * depth * width,
            bytes_accessed=2 * weight.size + 8 * xs[0].size,
            transcendentals=0,
        ),
        compiler_params=pltpu.CompilerParams(vmem_limit_bytes=PROJECT_VMEM),
        name="project_other" if other else "project_own",
    )(*operands)


def base_inverses(lowers):
    count = CHUNK // BASE
    tiles = BASE // 8
    lane_block = iota((8, CHUNK), 1) // BASE
    inside = iota((8, CHUNK), 1) % BASE
    packed, results = [], []
    for lower in lowers:
        pack, result = [], []
        for t in range(tiles):
            tile = jnp.zeros((8, CHUNK), F32)
            for b in range(count):
                start = b * BASE + 8 * t
                tile = jnp.where(lane_block == b, lower[start : start + 8], tile)
            pack.append(tile)
            result.append(jnp.where(inside == iota((8, CHUNK), 0) + 8 * t, 1.0, 0.0))
        packed.append(pack)
        results.append(result)
    for j in range(BASE - 1):
        source = lane_block * BASE + j
        for pack, result in zip(packed, results):
            row = jnp.broadcast_to(result[j // 8][j % 8 : j % 8 + 1], (8, CHUNK))
            for t in range((j + 1) // 8, tiles):
                column = jnp.take_along_axis(pack[t], source, axis=1)
                result[t] = result[t] - column * row
    block = iota((BASE, CHUNK), 1) // BASE
    totals = []
    for result in results:
        side = jnp.concatenate(result, axis=0)
        totals.append(
            jnp.concatenate([jnp.where(block == b, side, 0.0) for b in range(count)], axis=0)
        )
    return totals


def odd_blocks(value, size):
    return jnp.concatenate([value[r : r + size] for r in range(size, CHUNK, 2 * size)], axis=0)


def between(even, odd, size):
    blocks = []
    for r in range(0, CHUNK // 2, size):
        blocks += [even[r : r + size], odd[r : r + size]]
    return jnp.concatenate(blocks, axis=0)


def inverses(lowers):
    totals = base_inverses(lowers)
    row, column = iota((CHUNK // 2, CHUNK), 0), iota((CHUNK // 2, CHUNK), 1)
    blank = jnp.zeros((CHUNK // 2, CHUNK), BF16)
    size = BASE
    while size < CHUNK:
        inside = column // size == 2 * (row // size)
        parts = [halves(total) for total in totals]
        corners = [halves(jnp.where(inside, odd_blocks(lower, size), 0.0)) for lower in lowers]
        inner = [halves(dot3_stacked(c, p)) for c, p in zip(corners, parts)]
        for i, total in enumerate(totals):
            left = [odd_blocks(part, size) for part in parts[i]]
            right = [between(blank, part, size) for part in inner[i]]
            odd = odd_blocks(total, size) - dot3_stacked(left, right)
            even = jnp.concatenate([total[r : r + size] for r in range(0, CHUNK, 2 * size)], axis=0)
            totals[i] = between(even, odd, size)
        size *= 2
    return totals


def activated(extended, slot, message, block, f, half, taps, first):
    rows = CHUNK
    lanes = slice(half * HEAD, (half + 1) * HEAD)
    rim = message[4 * block + f, rows:, lanes].astype(F32)
    before = message[4 * jnp.maximum(block - 1, 0) + f, rows - RIM : rows, lanes].astype(F32)
    extended[slot, :RIM] = jnp.where(block == 0, rim, before)
    extended[slot, RIM:] = message[4 * block + f, :rows, lanes].astype(F32)
    weights = taps[:, pl.ds(pl.multiple_of(first * HEAD, HEAD), HEAD)].astype(F32)
    total = jnp.zeros((rows, HEAD), F32)
    for tap in range(KERNEL):
        begin = RIM - (KERNEL - 1) + tap
        total = total + weights[tap : tap + 1] * extended[slot, begin : begin + rows]
    middle = 0.5 * total
    return middle + middle * jnp.tanh(middle)


def unit(vectors):
    return vectors * lax.rsqrt(jnp.sum(vectors * vectors, axis=-1, keepdims=True) + 1e-06)


def prepare_kernel(seg_product, place, rate, bias, taps, message, *rest):
    carry_out, add_out, high_out, low_out, ratio_out, growth_out, key_high, key_low = rest[:8]
    final = rest[8]
    if seg_product:
        product_out, extended, state, product = rest[9:]
    else:
        extended, state = rest[9:]
    j = place[0]
    rows = CHUNK
    blocks = carry_out.shape[0]

    row, column = iota((rows, rows), 0), iota((rows, rows), 1)
    strict, within = row > column, row >= column
    eye = jnp.where(row == column, 1.0, 0.0)
    upper = jnp.where(row <= column, 1.0, 0.0)
    lower_eye = jnp.concatenate([jnp.where(within, 1.0, 0.0), eye], axis=0)
    heads = [SPLIT * h + j for h in range(PAIR)]
    state[...] = jnp.zeros_like(state)
    if seg_product:
        product[...] = jnp.broadcast_to(eye, product.shape)

    def gate_tables(block):
        decay_rows, strength_rows = [], []
        for u in range(UNITS):
            h, a = u // 2, u % 2
            head = 2 * heads[h] + a
            lanes = slice(a * HEAD, (a + 1) * HEAD)

            def gate(f):
                parts = message[4 * block + f, rows : rows + EXTRA, lanes].astype(F32)
                return (parts[0:1] + parts[1:2]) + parts[2:3]

            strength_rows.append(1.0 / (1.0 + jnp.exp(-gate(h))))
            shift = gate(2 + h) + bias[head]
            soft = jnp.maximum(shift, 0.0) + jnp.log1p(jnp.exp(-jnp.abs(shift)))
            decay_rows.append(-rate[head] * soft)
        return jnp.concatenate(decay_rows + strength_rows, axis=0)

    def several(index, _):
        group = [GROUPED * index + i for i in range(GROUPED)]
        tables = jnp.concatenate([gate_tables(block) for block in group], axis=0)
        sums = jnp.dot(tables, upper, precision=HIGHEST, preferred_element_type=F32)
        turned = lax.dot_general(
            lower_eye, tables, (((1,), (1,)), ((), ())), precision=HIGHEST, preferred_element_type=F32
        )
        keys, keys_t, scores = [], [], []
        for i, block in enumerate(group):
            for h in range(PAIR):
                slot = (PAIR + UNITS) * i + h
                key = unit(activated(extended, slot, message, block, 1, h, taps, HK + heads[h]))
                keys.append(key)
                keys_t.append(key.T)
                parts = halves(keys_t[-1])
                key_high[block, h], key_low[block, h] = parts
                scores.append(dot3_stacked(halves(key), parts))
        growths, strengths, lasts, trailings, lowers = [], [], [], [], []
        for i, block in enumerate(group):
            growth_all = jnp.exp(turned[:rows, 2 * UNITS * i : 2 * UNITS * (i + 1)])
            growth_out[block] = growth_all
            for u in range(UNITS):
                at = 2 * UNITS * i + u
                cum_c = turned[:rows, at : at + 1]
                strength = turned[rows:, at + UNITS : at + UNITS + 1]
                cum_r = sums[at : at + 1]
                last = sums[at : at + 1, rows - 1 : rows]
                ratio = jnp.where(within, jnp.exp(jnp.minimum(cum_c - cum_r, 0.0)), 0.0)
                ratio_out[block, u] = ratio
                growths.append(growth_all[:, u : u + 1])
                strengths.append(strength)
                lasts.append(last)
                trailings.append(jnp.exp(jnp.minimum(last - cum_r, 0.0)))
                score = scores[PAIR * i + u // 2]
                lowers.append(jnp.where(strict, strength * ratio * score, 0.0))
        solves = inverses(lowers)
        weighted = []
        for i, block in enumerate(group):
            for u in range(UNITS):
                h, a, at = u // 2, u % 2, UNITS * i + u
                slot = (PAIR + UNITS) * i + PAIR + u
                first = 2 * HK + 2 * heads[h] + a
                value = activated(extended, slot, message, block, 2 + h, a, taps, first)
                scaled = jnp.concatenate(
                    [(strengths[at] * growths[at]) * keys[PAIR * i + h], strengths[at] * value],
                    axis=1,
                )
                weighted.append(halves(dot3(halves(solves[at]), halves(scaled))))
                high_out[block, u], low_out[block, u] = weighted[at]
        carries, adds = [], []
        for i, block in enumerate(group):
            for u in range(UNITS):
                at = UNITS * i + u
                left = trailings[at] * keys_t[PAIR * i + u // 2]
                mixed = dot3(halves(left), weighted[at])
                carry = jnp.exp(lasts[at]) * eye - mixed[:, :HEAD]
                carry_out[block, u] = carry
                add_out[block, u] = mixed[:, HEAD:]
                carries.append(halves(carry))
                adds.append(mixed[:, HEAD:])
        for i in range(GROUPED):
            for u in range(UNITS):
                at = UNITS * i + u
                state[u] = dot3_stacked(carries[at], halves(state[u])) + adds[at]
                if seg_product:
                    product[u] = dot3(carries[at], halves(product[u]))
        return 0

    lax.fori_loop(0, blocks // GROUPED, several, 0)
    final[...] = state[...].astype(final.dtype)
    if seg_product:
        product_out[...] = product[...].astype(product_out.dtype)


def prepare(place, rate, bias, message, taps, seg_product):
    blocks = message.shape[0] // 4
    rows = message.shape[1] - EXTRA
    assert rows == CHUNK
    state_shape = (UNITS, HEAD, HEAD)
    streams = [
        (state_shape, F32),
        (state_shape, F32),
        ((UNITS, rows, 2 * HEAD), BF16),
        ((UNITS, rows, 2 * HEAD), BF16),
        ((UNITS, rows, rows), F32),
        ((rows, 2 * UNITS), F32),
        ((PAIR, HEAD, rows), BF16),
        ((PAIR, HEAD, rows), BF16),
    ]
    out_shape = [jax.ShapeDtypeStruct((blocks,) + shape, dtype) for shape, dtype in streams]
    out_shape.append(jax.ShapeDtypeStruct(state_shape, BF16))
    scratch = [
        pltpu.VMEM(((PAIR + UNITS) * GROUPED, RIM + rows, HEAD), F32),
        pltpu.VMEM(state_shape, F32),
    ]
    if seg_product:
        out_shape.append(jax.ShapeDtypeStruct(state_shape, F32))
        scratch.append(pltpu.VMEM(state_shape, F32))
    scalars = pl.BlockSpec(memory_space=pltpu.SMEM)
    vectors = pl.BlockSpec(memory_space=pltpu.VMEM)
    return pl.pallas_call(
        lambda *refs: prepare_kernel(seg_product, *refs),
        in_specs=[scalars] * 3 + [vectors] * 2,
        out_specs=[vectors] * len(out_shape),
        out_shape=out_shape,
        scratch_shapes=scratch,
        compiler_params=pltpu.CompilerParams(vmem_limit_bytes=VMEM_LIMIT),
        name="prepare",
    )(place, rate, bias, taps, message)


def local_kernel(place, message, taps, high, low, ratio, growth, key_high, key_low, *rest):
    query_out, base_out, extended = rest
    heads = [SPLIT * h + place[0] for h in range(PAIR)]

    def one(block, _):
        queries, scores = [], []
        for h in range(PAIR):
            vectors = unit(activated(extended, h, message, block, 0, h, taps, heads[h]))
            queries.append(vectors * HEAD ** (-0.5))
            scores.append(dot3(halves(queries[h]), (key_high[block, h], key_low[block, h])))
        mixed = []
        for u in range(UNITS):
            mixing = ratio[block, u] * scores[u // 2]
            mixed.append(dot3(halves(mixing), (high[block, u], low[block, u])))
        for u in range(UNITS):
            query_out[block, u] = (
                growth[block, :, u : u + 1] * queries[u // 2] - mixed[u][:, :HEAD]
            )
            base_out[block, u] = mixed[u][:, HEAD:]
        return 0

    lax.fori_loop(0, query_out.shape[0], one, 0)


def local(place, message, taps, parts):
    blocks = message.shape[0] // 4
    rows = message.shape[1] - EXTRA
    shape = (blocks, UNITS, rows, HEAD)
    vectors = pl.BlockSpec(memory_space=pltpu.VMEM)
    flops = blocks * UNITS * 2 * 3 * rows * rows * 3 * HEAD
    return pl.pallas_call(
        local_kernel,
        in_specs=[pl.BlockSpec(memory_space=pltpu.SMEM)] + [vectors] * (2 + len(parts)),
        out_specs=[vectors, vectors],
        out_shape=[jax.ShapeDtypeStruct(shape, F32)] * 2,
        scratch_shapes=[pltpu.VMEM((PAIR, RIM + rows, HEAD), F32)],
        cost_estimate=pl.CostEstimate(
            flops=flops, bytes_accessed=12 << 20, transcendentals=message.size
        ),
        compiler_params=pltpu.CompilerParams(vmem_limit_bytes=VMEM_LIMIT),
        name="local",
    )(place, message, taps, *parts)


def read_kernel(place, carry, add, query, base, start, gain, *rest):
    outs, (stage, state) = rest[:-2], rest[-2:]
    state[...] = start[...].astype(F32)
    for block in range(carry.shape[0]):
        slot = jnp.bitwise_xor(block, place[0])
        for u in range(UNITS):
            left = jnp.concatenate([carry[block, u], query[block, u]], axis=0)
            both = dot3(halves(left), halves(state[u]))
            state[u] = both[:HEAD] + add[block, u]
            reads = both[HEAD:] + base[block, u]
            mean = jnp.mean(reads * reads, axis=-1, keepdims=True)
            stage[slot, :, u * HEAD : (u + 1) * HEAD] = (
                reads / jnp.sqrt(mean + 1e-06) * gain[...]
            ).astype(BF16)
    for k, out in enumerate(outs):
        out[...] = stage[k]


def read(place, carry, add, query, base, start, gain):
    blocks, _, rows, _ = query.shape
    vectors = pl.BlockSpec(memory_space=pltpu.VMEM)
    return pl.pallas_call(
        read_kernel,
        in_specs=[pl.BlockSpec(memory_space=pltpu.SMEM)] + [vectors] * 6,
        out_specs=[vectors] * blocks,
        out_shape=[jax.ShapeDtypeStruct((rows, UNITS * HEAD), BF16)] * blocks,
        scratch_shapes=[
            pltpu.VMEM((blocks, rows, UNITS * HEAD), BF16),
            pltpu.VMEM(start.shape, F32),
        ],
        compiler_params=pltpu.CompilerParams(vmem_limit_bytes=VMEM_LIMIT),
        name="read",
    )(place, carry, add, query, base, start, gain)


def assemble_kernel(place, *refs):
    out = refs[-1]
    width = 2 * HEAD
    for k, piece in enumerate(refs[:-1]):
        source = jnp.bitwise_xor(place[0], k)
        for h in range(PAIR):
            first = pl.multiple_of((h * SPLIT + source) * width, width)
            out[0, :, pl.ds(first, width)] = piece[:, h * width : (h + 1) * width]


def assemble(place, pieces):
    rows = pieces[0].shape[0]
    return pl.pallas_call(
        assemble_kernel,
        in_specs=[pl.BlockSpec(memory_space=pltpu.SMEM)]
        + [pl.BlockSpec(memory_space=pltpu.VMEM)] * len(pieces),
        out_specs=pl.BlockSpec(memory_space=pltpu.VMEM),
        out_shape=jax.ShapeDtypeStruct((1, rows, HV * HEAD), BF16),
        compiler_params=pltpu.CompilerParams(vmem_limit_bytes=VMEM_LIMIT),
        name="assemble",
    )(place, *pieces)


def messages_direct(tokens, qkv_weight, gate_weight, seq_count):
    me = lax.axis_index("fsdp")
    rim_rows = tokens[tokens.shape[0] - RIM :]
    far = swapped(tokens, "fsdp", 2)
    near = swapped(tokens, "fsdp", 1)
    rim_0 = shifted(rim_rows, ("seg", "sq"), [(i, i + 1) for i in range(seq_count - 1)])
    rim_1 = swapped(rim_0, "fsdp", 1)
    rim_2 = swapped(rim_0, "fsdp", 2)
    gate_t = gate_weight.T
    place = me.astype(jnp.int32)[None]
    message, weight, gate_t = project(
        place,
        (in_hbm(tokens), near),
        (rim_0, rim_1),
        in_hbm(gate_t),
        in_hbm(qkv_weight),
        None,
    )
    third = swapped(far, "fsdp", 1)
    rim_3 = swapped(rim_2, "fsdp", 1)
    message = project(place, (far, third), (rim_2, rim_3), gate_t, weight, message)[0]
    message = message.reshape((SPLIT * 4,) + message.shape[2:])
    return lax.all_to_all(message, ("sq", "fsdp"), 0, 0, tiled=True)


def messages_staged(tokens, qkv_weight, gate_weight, seq_count):
    length = tokens.shape[0]
    every = lax.all_gather(tokens, "fsdp", axis=0)
    mixed = jnp.einsum("ild,dc->ilc", every, qkv_weight, preferred_element_type=F32).astype(BF16)
    mixed = lax.all_to_all(mixed, "fsdp", 0, 2, tiled=True)[0]
    rim = shifted(
        mixed[length - RIM :], ("seg", "sq"), [(i, i + 1) for i in range(seq_count - 1)]
    )
    gates = jnp.dot(tokens, gate_weight, preferred_element_type=F32)
    high = lax.reduce_precision(gates, 8, 7)
    middle = lax.reduce_precision(gates - high, 8, 7)
    parts = jnp.stack([high, middle, (gates - high) - middle]).astype(BF16)
    parts = parts.reshape(3, length, 4, SPLIT, 2).transpose(3, 2, 0, 4, 1)
    parts = parts.reshape(SPLIT, 4, 3, 2 * length)

    def by_target(rows):
        count = rows.shape[0]
        query_key = rows[:, : 2 * HK * HEAD].reshape(count, 2, PAIR, SPLIT, HEAD)
        query_key = query_key.transpose(3, 1, 0, 2, 4).reshape(SPLIT, 2, count, 2 * HEAD)
        value = rows[:, 2 * HK * HEAD :].reshape(count, PAIR, SPLIT, 2 * HEAD)
        return jnp.concatenate([query_key, value.transpose(2, 1, 0, 3)], axis=1)

    rim = by_target(rim)[:, :, 3:]
    message = jnp.concatenate([by_target(mixed), parts, rim], axis=2)
    message = lax.all_to_all(message, "sq", 0, 0, tiled=True)
    return message.reshape((SPLIT * 4,) + message.shape[2:])


def layer(inputs, qkv_weight, gate_weight, conv_weight, head_rate, dt_bias, norm_gain):
    segments = lax.axis_size("seg")
    tokens = inputs[0]
    build = messages_direct if lax.axis_size("fsdp") == 4 else messages_staged
    message = build(tokens, qkv_weight, gate_weight, segments * SPLIT)
    place = lax.axis_index("sq").astype(jnp.int32)[None]
    outs = prepare(place, head_rate, dt_bias, message, conv_weight, segments > 2)
    carry, add, parts, final = outs[0], outs[1], outs[2:8], outs[8]
    onward = [(i, i + 1) for i in range(segments - 1)]
    start = jnp.zeros_like(final)
    if segments == 2:
        start = shifted(final, "seg", onward)
    elif segments > 2:
        for _ in range(segments - 1):
            ahead = jnp.einsum("hij,hjk->hik", outs[9], start.astype(F32), precision=HIGHEST)
            start = shifted((ahead + final.astype(F32)).astype(BF16), "seg", onward)
    query, base = local(place, message, conv_weight, parts)
    pieces = read(place, carry, add, query, base, start, norm_gain[None])
    received = [pieces[0]] + [swapped(pieces[k], "sq", k) for k in range(1, SPLIT)]
    return assemble(place, received)


def solution(mesh):
    seq, fsdp = mesh.shape["seq"], mesh.shape["fsdp"]
    parts = Mesh(mesh.devices.reshape(seq // SPLIT, SPLIT, fsdp), ("seg", "sq", "fsdp"))
    split = P("fsdp", ("seg", "sq"), None)
    in_specs = (split, P(None, "fsdp"), P(), P(), P(), P(), P())
    return jax.shard_map(layer, mesh=parts, in_specs=in_specs, out_specs=split, check_vma=False)
```
